128 devices in a mesh: blk: 16 (over y, z_lo, core), col: 8 (over x, z_hi).
Axes of the slice: x: 4, y: 4, z: 4 (z_hi: 2, z_lo: 2; z = z_hi * 2 + z_lo), core: 2. Of those that a mesh axis runs over, the one named last changes fastest.
Arguments:
- three_index: float32 [4096, 12, 4096], P('blk', None, 'col'), may hold values from -6 to 6
- coefficients: float32 [4096, 1024], P('col', 'blk'), may hold values from -0.0078125 to 0.0078125
Outputs:
- exchange_matrix: float32 [4096, 4096], P(('blk', 'col'))
The draws below stay inside these ranges and needn't reach their ends.
All inputs are finite; a program needn't handle non-finite values.
Results may differ from the reference program's by a relative error of at most 0.000065.
Values sent between devices are 32-bit elements; how exact they have to be, the bound alone decides.
No kernel may reach another device: no remote copies, remote signals or barrier semaphores. Data moves between devices by JAX's collectives and lax.ppermute only.
A program may use at most 128 MiB of HBM per device.

```python
import jax
import jax.numpy as jnp
from jax import lax

NBF = 4096
NOCC = 1024
AUX = 12


def steps_of(own_key, shape, cuts, least, high):
    def one(position, parts):
        draws = jax.random.uniform(jax.random.fold_in(jax.random.fold_in(own_key, 6), position), (parts,), jnp.float32, least / len(cuts), high / len(cuts))
        return jnp.repeat(jnp.exp(draws), shape[position] // parts).reshape((-1,) + (1,) * (len(shape) - position - 1))

    gain = one(*cuts[0])
    for cut in cuts[1:]:
        gain = gain * one(*cut)
    return gain


def centred(stream_key, dims, spread, bound, split=(), kind=jnp.bfloat16):
    result = jax.random.normal(stream_key, dims, jnp.float32) * spread
    if len(split) > 0:
        result = steps_of(stream_key, dims, split, -0.22, 0.18) * result
    return jnp.clip(result, min=-bound, max=bound).astype(kind)


def setup_inputs(seed: int = 0) -> dict:
    arg_keys = jax.random.split(jax.random.key(seed), 3)
    three_index = centred(arg_keys[0], (NBF, AUX, NBF), 1.0, 6.0, ((0, 16), (2, 8)), jnp.float32)
    coefficients = centred(arg_keys[1], (NBF, NOCC), (NBF * (AUX * NOCC) ** 0.5) ** -0.5, 0.0078125, ((0, 8), (1, 16)), jnp.float32)
    return {"three_index": three_index, "coefficients": coefficients}


def reference(three_index, coefficients):
    flattened = three_index.reshape(NBF * AUX, NBF)
    half_x = jnp.dot(flattened, coefficients, precision=lax.Precision.HIGHEST, preferred_element_type=jnp.float32)
    half_x = half_x.reshape(NBF, AUX * NOCC)
    return jnp.dot(half_x, half_x.T, precision=lax.Precision.HIGHEST, preferred_element_type=jnp.float32)
```

```python
import jax
import jax.numpy as jnp
from jax import lax
from jax.sharding import PartitionSpec as P

Y, ZL, CORES, X, ZH = 4, 2, 2, 4, 2
HIGH = lax.Precision.HIGH
X_GROUPS = [[x * ZH + zh for x in range(X)] for zh in range(ZH)]


def block_of(y, zl, core):
    return ((y % Y) * ZL + zl % ZL) * CORES + core % CORES


def upper(y):
    return (y % Y) // 2


def next_row(y, zl, core):
    return y + 1, zl, core


def next_across(y, zl, core):
    return y + 1, 1 - zl, (core + zl + upper(y)) % 2


def previous_row(y, zl, core):
    return y - 1, zl, (core + upper(y)) % 2


def places():
    return [(y, zl, core) for y in range(Y) for zl in range(ZL) for core in range(CORES)]


def fetched(value, source_of):
    route = [(block_of(*source_of(*at)), block_of(*at)) for at in places()]
    return lax.ppermute(value, "blk", route)


def delivered(value, target_of):
    route = [(block_of(*at), block_of(*target_of(*at))) for at in places()]
    return lax.ppermute(value, "blk", route)


def other_core(y, zl, core):
    return y, zl, 1 - core


def over_to_across(y, zl, core):
    return y, 1 - zl, (core + zl + upper(y)) % 2


def product(left, right):
    return lax.dot_general(
        left, right, (((1,), (1,)), ((), ())), precision=HIGH, preferred_element_type=jnp.float32
    )


def all_orbitals(coefficients):
    mine = coefficients.T
    x = lax.axis_index("col") // ZH
    ring = {}
    for step in range(1, X):
        route = [(((t + step) % X) * ZH + zh, t * ZH + zh) for t in range(X) for zh in range(ZH)]
        ring[step] = lax.ppermute(mine, "col", route)
    order = [ring[1], ring[2], ring[3], mine]
    twice = jnp.stack(order + order[:3])
    by_x = lax.dynamic_slice(twice, (X - 1 - x, 0, 0), (X,) + mine.shape)
    joined = by_x.transpose(1, 0, 2).reshape(mine.shape[0], X * mine.shape[1])
    return lax.all_gather(joined, "blk", axis=0, tiled=True)


def on_device(three_index, coefficients):
    rows, aux, _ = three_index.shape
    by_aux = three_index.transpose(1, 0, 2)
    blk, col = lax.axis_index("blk"), lax.axis_index("col")
    y, zl, core = blk // (ZL * CORES), (blk // CORES) % ZL, blk % CORES
    zh = col % ZH
    swap_zh = [(x * ZH + 1 - h, x * ZH + h) for x in range(X) for h in range(ZH)]

    orbitals = all_orbitals(coefficients)
    half = orbitals.shape[0] // ZH
    kept = lax.dynamic_slice(orbitals, (zh * half, 0), (half, orbitals.shape[1]))
    sent = lax.dynamic_slice(orbitals, ((1 - zh) * half, 0), (half, orbitals.shape[1]))

    tiles = None
    for chunk in range(aux // X):
        part = lax.all_to_all(
            by_aux[X * chunk : X * (chunk + 1)],
            "col",
            split_axis=0,
            concat_axis=2,
            tiled=True,
            axis_index_groups=X_GROUPS,
        )[0]
        arrived = lax.ppermute(product(part, sent), "col", swap_zh)
        own = product(part, kept) + arrived
        other = fetched(own, other_core)
        below = fetched(own, next_row)
        above = fetched(own, previous_row)
        across = fetched(below, over_to_across)
        pair = jnp.concatenate([own, other])
        terms = (
            product(own, pair),
            product(below, pair),
            product(across, jnp.concatenate([pair, below])),
            product(above, jnp.concatenate([below, across])),
        )
        tiles = terms if tiles is None else tuple(a + b for a, b in zip(tiles, terms))

    own_t, below_t, across_t, above_t = tiles
    flip = lambda t: t.T
    cut = lambda t, k: t[:, k * rows : (k + 1) * rows]
    slabs = [
        own_t, flip(cut(below_t, 0)), flip(cut(across_t, 0)),
        flip(cut(below_t, 1)), flip(cut(across_t, 1)),
        below_t, flip(cut(across_t, 2)), flip(cut(above_t, 0)),
        across_t, flip(cut(above_t, 1)),
        above_t,
    ]
    whole = jnp.concatenate(slabs, axis=1)
    shares = lax.axis_size("col")
    split = whole.reshape(shares, rows // shares, whole.shape[1])
    summed = lax.all_to_all(split, "col", split_axis=0, concat_axis=0, tiled=True).sum(0)

    def span(first, count):
        return summed[:, first * rows : (first + count) * rows]

    def columns(at):
        other_at = other_core(*at)
        return {"own": at, "other": other_at, "below": next_row(*at),
                "across": next_across(*at), "above": previous_row(*at)}

    here = (y, zl, core)
    partner = other_core(*here)
    of_below = (y - 1, zl, core)
    of_across = (y - 1, 1 - zl, (core + (1 - zl) + upper(y - 1)) % 2)
    of_above = (y + 1, zl, (core + upper(y + 1)) % 2)
    arrivals = [
        (span(0, 4), here, ("own", "other", "below", "across")),
        (delivered(span(4, 2), other_core), partner, ("below", "across")),
        (delivered(span(6, 4), next_row), of_below, ("own", "other", "across", "above")),
        (delivered(span(10, 4), next_across), of_across, ("own", "other", "below", "above")),
        (delivered(span(14, 2), previous_row), of_above, ("below", "across")),
    ]
    result = jnp.zeros(summed.shape, jnp.float32)
    for slab, source, names in arrivals:
        at = columns(source)
        for k, name in enumerate(names):
            column = block_of(*at[name]) * rows
            piece = slab[:, k * rows : (k + 1) * rows]
            result = lax.dynamic_update_slice(result, piece, (jnp.int32(0), column))
    return result


def solution(mesh):
    return jax.shard_map(
        on_device,
        mesh=mesh,
        in_specs=(P("blk", None, "col"), P("col", "blk")),
        out_specs=P(("blk", "col"), None),
        check_vma=False,
    )
```

```python
import functools

import jax
import jax.numpy as jnp
import numpy as np
from jax import lax
from jax.experimental import pallas as pl
from jax.experimental.pallas import tpu as pltpu
from jax.sharding import PartitionSpec as P

Y, ZL, CORES, X, ZH = 4, 2, 2, 4, 2
X_GROUPS = [[x * ZH + zh for x in range(X)] for zh in range(ZH)]
OWN, OTHER, BELOW, ABOVE, ACROSS = range(5)
EARLY = [(OWN, OWN), (OWN, OTHER), (OWN, BELOW), (OTHER, BELOW),
         (BELOW, OWN), (BELOW, OTHER), (BELOW, ABOVE), (ABOVE, BELOW)]
LATE = [(OWN, ACROSS), (OTHER, ACROSS), (BELOW, ACROSS), (ABOVE, ACROSS),
        (ACROSS, OWN), (ACROSS, OTHER), (ACROSS, BELOW), (ACROSS, ABOVE)]


def block_of(y, zl, core):
    return ((y % Y) * ZL + zl % ZL) * CORES + core % CORES


def upper(y):
    return (y % Y) // 2


def itself(y, zl, core):
    return y, zl, core


def other_core(y, zl, core):
    return y, zl, 1 - core


def next_row(y, zl, core):
    return y + 1, zl, core


def previous_row(y, zl, core):
    return y - 1, zl, (core + upper(y)) % 2


def next_across(y, zl, core):
    return y + 1, 1 - zl, (core + zl + upper(y)) % 2


def over_to_across(y, zl, core):
    return y, 1 - zl, (core + zl + upper(y)) % 2


RELATED = [itself, other_core, next_row, previous_row, next_across]


def places():
    return [(y, zl, core) for y in range(Y) for zl in range(ZL) for core in range(CORES)]


def fetched(value, source_of):
    route = [(block_of(*source_of(*at)), block_of(*at)) for at in places()]
    return lax.ppermute(value, "blk", route)


def delivered(value, target_of):
    route = [(block_of(*at), block_of(*target_of(*at))) for at in places()]
    return lax.ppermute(value, "blk", route)


def column_table():
    table = np.zeros((len(places()), len(EARLY) + len(LATE)), np.int32)
    slot = 0
    for tiles in (EARLY, LATE):
        for row in range(5):
            for left, right in tiles:
                if left != row:
                    continue
                for at in places():
                    target = block_of(*RELATED[row](*at))
                    table[target, slot] = block_of(*RELATED[right](*at))
                slot += 1
    return table


def high_and_low(value):
    high = value.astype(jnp.bfloat16)
    return high, (value - high.astype(jnp.float32)).astype(jnp.bfloat16)


def dot(left, right):
    return lax.dot_general(
        left, right, (((1,), (1,)), ((), ())), preferred_element_type=jnp.float32
    )


def transform_kernel(place, part, orbitals, out, high, low):
    width = part.shape[-1]

    @pl.when(pl.program_id(0) == 0)
    def _():
        for x in range(X):
            high[:, x * width : (x + 1) * width], low[:, x * width : (x + 1) * width] = (
                high_and_low(part[x, 0])
            )

    total = jnp.zeros(out.shape, jnp.float32)
    for x in range(X):
        slot = lax.rem(x - place[0] + X, X)
        block = orbitals[:, pl.ds(slot, 1)]
        c_high, c_low = high_and_low(block.reshape(out.shape[1], width))
        b_high = high[:, x * width : (x + 1) * width]
        b_low = low[:, x * width : (x + 1) * width]
        total += dot(b_high, c_high) + (dot(b_high, c_low) + dot(b_low, c_high))
    out[...] = total


def transformed(part, index, orbitals, place, half):
    rows, width = part.shape[2:]
    blocks, _, each, _ = orbitals.shape
    steps, run = 2, blocks // 4
    columns = run * each
    return pl.pallas_call(
        transform_kernel,
        grid_spec=pltpu.PrefetchScalarGridSpec(
            num_scalar_prefetch=1,
            grid=(steps,),
            in_specs=[
                pl.BlockSpec((X, 1, rows, width), lambda j, s: (0, index, 0, 0)),
                pl.BlockSpec((run, X, each, width), lambda j, s: (s[1] * 2 + j, 0, 0, 0)),
            ],
            out_specs=pl.BlockSpec((rows, columns), lambda j, s: (0, j)),
            scratch_shapes=[pltpu.VMEM((rows, X * width), jnp.bfloat16)] * 2,
        ),
        out_shape=jax.ShapeDtypeStruct((rows, steps * columns), jnp.float32),
        compiler_params=pltpu.CompilerParams(vmem_limit_bytes=32 << 20),
        cost_estimate=pl.CostEstimate(
            flops=6 * rows * X * width * steps * columns, bytes_accessed=8 << 20, transcendentals=0
        ),
        name="transform",
    )(jnp.stack([place, half]), part, orbitals)


def gram_kernel(count, more, left_of, right_of, *refs):
    blocks, refs = refs[:count], refs[count:]
    if more:
        so_far, refs = refs[0], refs[1:]
    out, lefts, rights = refs
    depth = blocks[0].shape[1]
    step = pl.program_id(0)

    @pl.when(step == 0)
    def _():
        for k, block in enumerate(blocks):
            high, low = high_and_low(block[...])
            for ref, order in ((lefts, (high, high, low)), (rights, (high, low, high))):
                for piece, value in enumerate(order):
                    ref[k, :, piece * depth : (piece + 1) * depth] = value

    tile = dot(lefts[left_of[step]], rights[right_of[step]]).reshape(out.shape)
    out[...] = so_far[...] + tile if more else tile


def gram(blocks, pairs, shares, so_far):
    rows, depth = blocks[0].shape
    count = len(blocks)
    tiles = len(pairs)
    more = so_far is not None
    whole = pl.BlockSpec((rows, depth), lambda t, *s: (0, 0))
    tile = pl.BlockSpec((shares, 1, rows // shares, rows), lambda t, *s: (0, t, 0, 0))
    shape = jax.ShapeDtypeStruct((shares, tiles, rows // shares, rows), jnp.float32)
    order = np.array(pairs, np.int32)
    return pl.pallas_call(
        functools.partial(gram_kernel, count, more),
        grid_spec=pltpu.PrefetchScalarGridSpec(
            num_scalar_prefetch=2,
            grid=(tiles,),
            in_specs=[whole] * count + [tile] * more,
            out_specs=tile,
            scratch_shapes=[pltpu.VMEM((count, rows, 3 * depth), jnp.bfloat16)] * 2,
        ),
        out_shape=shape,
        input_output_aliases={2 + count: 0} if more else {},
        compiler_params=pltpu.CompilerParams(vmem_limit_bytes=32 << 20),
        cost_estimate=pl.CostEstimate(
            flops=6 * tiles * rows * rows * depth, bytes_accessed=6 << 20, transcendentals=0
        ),
        name="gram",
    )(order[:, 0], order[:, 1], *blocks, *([so_far] if more else []))


def assemble_kernel(table, *refs):
    *groups, out = refs
    slot = 0
    for group in groups:
        for k in range(group.shape[0]):
            width = group.shape[2]
            at = pl.multiple_of(table[slot] * width, width)
            out[:, pl.ds(at, width)] = group[k]
            slot += 1


def assembled(table, groups, columns):
    return pl.pallas_call(
        assemble_kernel,
        in_specs=[pl.BlockSpec(memory_space=pltpu.SMEM)]
        + [pl.BlockSpec(memory_space=pltpu.VMEM)] * len(groups),
        out_specs=pl.BlockSpec(memory_space=pltpu.VMEM),
        out_shape=jax.ShapeDtypeStruct((groups[0].shape[1], columns), jnp.float32),
        cost_estimate=pl.CostEstimate(flops=0, bytes_accessed=1 << 20, transcendentals=0),
        name="assemble",
    )(table, *groups)


def all_orbitals(coefficients):
    mine = coefficients.T
    ring = [mine]
    for step in range(1, X):
        route = [(((t + step) % X) * ZH + zh, t * ZH + zh) for t in range(X) for zh in range(ZH)]
        ring.append(lax.ppermute(mine, "col", route))
    return lax.all_gather(jnp.stack(ring), "blk", axis=0, tiled=False)


def on_device(three_index, coefficients):
    rows, aux, width = three_index.shape
    by_aux = three_index.transpose(1, 0, 2)
    blk, col = lax.axis_index("blk"), lax.axis_index("col")
    place, zh = col // ZH, col % ZH
    swap_zh = [(x * ZH + 1 - h, x * ZH + h) for x in range(X) for h in range(ZH)]
    shares = lax.axis_size("col")

    def over_x(part):
        moved = lax.all_to_all(
            part, "col", split_axis=0, concat_axis=0, tiled=True, axis_index_groups=X_GROUPS
        )
        return moved.reshape(X, part.shape[0] // X, rows, width)

    cut = aux - X
    parts = [over_x(by_aux[:cut]), over_x(by_aux[cut:])]
    orbitals = all_orbitals(coefficients)
    chunks = [(part, k) for part in parts for k in range(part.shape[1])]

    early = late = None
    for part, k in chunks:
        arrived = lax.ppermute(transformed(part, k, orbitals, place, 1 - zh), "col", swap_zh)
        own = transformed(part, k, orbitals, place, zh) + arrived
        other = fetched(own, other_core)
        below = fetched(own, next_row)
        above = fetched(own, previous_row)
        across = fetched(below, over_to_across)
        early = gram([own, other, below, above], EARLY, shares, early)
        late = gram([own, other, below, above, across], LATE, shares, late)

    def sent_home(tiles, pairs):
        summed = lax.all_to_all(tiles, "col", split_axis=0, concat_axis=0, tiled=True).sum(0)
        groups = []
        first = 0
        for row, target_of in enumerate(RELATED):
            count = sum(left == row for left, _ in pairs)
            if count:
                group = summed[first : first + count]
                groups.append(delivered(group, target_of) if row else group)
            first += count
        return groups

    groups = sent_home(early, EARLY) + sent_home(late, LATE)
    table = lax.dynamic_slice(jnp.asarray(column_table()), (blk, 0), (1, 16))[0]
    return assembled(table, groups, rows * lax.axis_size("blk"))


def solution(mesh):
    return jax.shard_map(
        on_device,
        mesh=mesh,
        in_specs=(P("blk", None, "col"), P("col", "blk")),
        out_specs=P(("blk", "col"), None),
        check_vma=False,
    )
```

```python
import functools

import jax
import jax.numpy as jnp
import numpy as np
from jax import lax
from jax.experimental import pallas as pl
from jax.experimental.pallas import tpu as pltpu
from jax.sharding import PartitionSpec as P

Y, ZL, CORES, X, ZH = 4, 2, 2, 4, 2
X_GROUPS = [[x * ZH + zh for x in range(X)] for zh in range(ZH)]
OWN, OTHER, BELOW, ABOVE, ACROSS = range(5)
EARLY = [(OWN, OWN), (OWN, OTHER), (OWN, BELOW), (OTHER, BELOW),
         (BELOW, OWN), (BELOW, OTHER), (BELOW, ABOVE), (ABOVE, BELOW)]
LATE = [(OWN, ACROSS), (OTHER, ACROSS), (BELOW, ACROSS), (ABOVE, ACROSS),
        (ACROSS, OWN), (ACROSS, OTHER), (ACROSS, BELOW), (ACROSS, ABOVE)]


def block_of(y, zl, core):
    return ((y % Y) * ZL + zl % ZL) * CORES + core % CORES


def upper(y):
    return (y % Y) // 2


def itself(y, zl, core):
    return y, zl, core


def other_core(y, zl, core):
    return y, zl, 1 - core


def next_row(y, zl, core):
    return y + 1, zl, core


def previous_row(y, zl, core):
    return y - 1, zl, (core + upper(y)) % 2


def next_across(y, zl, core):
    return y + 1, 1 - zl, (core + zl + upper(y)) % 2


def over_to_across(y, zl, core):
    return y, 1 - zl, (core + zl + upper(y)) % 2


RELATED = [itself, other_core, next_row, previous_row, next_across]


def places():
    return [(y, zl, core) for y in range(Y) for zl in range(ZL) for core in range(CORES)]


def fetched(value, source_of):
    route = [(block_of(*source_of(*at)), block_of(*at)) for at in places()]
    return lax.ppermute(value, "blk", route)


def delivered(value, target_of):
    route = [(block_of(*at), block_of(*target_of(*at))) for at in places()]
    return lax.ppermute(value, "blk", route)


def column_table():
    table = np.zeros((len(places()), len(EARLY) + len(LATE)), np.int32)
    slot = 0
    for tiles in (EARLY, LATE):
        for row in range(5):
            for left, right in tiles:
                if left != row:
                    continue
                for at in places():
                    target = block_of(*RELATED[row](*at))
                    table[target, slot] = block_of(*RELATED[right](*at))
                slot += 1
    return table


def high_and_low(value):
    high = value.astype(jnp.bfloat16)
    return high, (value - high.astype(jnp.float32)).astype(jnp.bfloat16)


def dot(left, right):
    return lax.dot_general(
        left, right, (((1,), (1,)), ((), ())), preferred_element_type=jnp.float32
    )


def transform_kernel(place, part, orbitals, out, high, low):
    width = part.shape[-1]

    @pl.when(pl.program_id(0) == 0)
    def _():
        for x in range(X):
            high[:, x * width : (x + 1) * width], low[:, x * width : (x + 1) * width] = (
                high_and_low(part[x, 0])
            )

    total = jnp.zeros(out.shape, jnp.float32)
    for x in range(X):
        slot = lax.rem(x - place[0] + X, X)
        block = orbitals[:, pl.ds(slot, 1)]
        c_high, c_low = high_and_low(block.reshape(out.shape[1], width))
        b_high = high[:, x * width : (x + 1) * width]
        b_low = low[:, x * width : (x + 1) * width]
        total += dot(b_high, c_high) + (dot(b_high, c_low) + dot(b_low, c_high))
    out[...] = total


def transformed(part, index, orbitals, place, half):
    rows, width = part.shape[2:]
    blocks, _, each, _ = orbitals.shape
    steps, run = 2, blocks // 4
    columns = run * each
    return pl.pallas_call(
        transform_kernel,
        grid_spec=pltpu.PrefetchScalarGridSpec(
            num_scalar_prefetch=1,
            grid=(steps,),
            in_specs=[
                pl.BlockSpec((X, 1, rows, width), lambda j, s: (0, index, 0, 0)),
                pl.BlockSpec((run, X, each, width), lambda j, s: (s[1] * 2 + j, 0, 0, 0)),
            ],
            out_specs=pl.BlockSpec((rows, columns), lambda j, s: (0, j)),
            scratch_shapes=[pltpu.VMEM((rows, X * width), jnp.bfloat16)] * 2,
        ),
        out_shape=jax.ShapeDtypeStruct((rows, steps * columns), jnp.float32),
        cost_estimate=pl.CostEstimate(
            flops=6 * rows * X * width * steps * columns, bytes_accessed=8 << 20, transcendentals=0
        ),
        name="transform",
    )(jnp.stack([place, half]), part, orbitals)


def gram_kernel(count, more, left_of, right_of, *refs):
    blocks, refs = refs[:count], refs[count:]
    if more:
        so_far, refs = refs[0], refs[1:]
    out, lefts, rights = refs
    depth = blocks[0].shape[1]
    chunks = count // lefts.shape[0]
    step = pl.program_id(0)

    @pl.when(step == 0)
    def _():
        for k, block in enumerate(blocks):
            high, low = high_and_low(block[...])
            at, first = k // chunks, k % chunks * 3
            for ref, order in ((lefts, (high, high, low)), (rights, (high, low, high))):
                for piece, value in enumerate(order, first):
                    ref[at, :, piece * depth : (piece + 1) * depth] = value

    shares, together, part, width = out.shape
    for k in range(together):
        at = step * together + k
        tile = dot(lefts[left_of[at]], rights[right_of[at]]).reshape(shares, part, width)
        out[:, k] = so_far[:, k] + tile if more else tile


def gram(blocks, pairs, shares, so_far=None):
    rows, depth = blocks[0][0].shape
    chunks = len(blocks[0])
    flat = [chunk for block in blocks for chunk in block]
    tiles, together = len(pairs), 2
    more = so_far is not None
    whole = pl.BlockSpec((rows, depth), lambda t, *s: (0, 0))
    tile = pl.BlockSpec((shares, together, rows // shares, rows), lambda t, *s: (0, t, 0, 0))
    shape = jax.ShapeDtypeStruct((shares, tiles, rows // shares, rows), jnp.float32)
    order = np.array(pairs, np.int32)
    return pl.pallas_call(
        functools.partial(gram_kernel, len(flat), more),
        grid_spec=pltpu.PrefetchScalarGridSpec(
            num_scalar_prefetch=2,
            grid=(tiles // together,),
            in_specs=[whole] * len(flat) + [tile] * more,
            out_specs=tile,
            scratch_shapes=[pltpu.VMEM((len(blocks), rows, 3 * chunks * depth), jnp.bfloat16)] * 2,
        ),
        out_shape=shape,
        input_output_aliases={2 + len(flat): 0} if more else {},
        cost_estimate=pl.CostEstimate(
            flops=6 * tiles * rows * rows * chunks * depth, bytes_accessed=6 << 20, transcendentals=0
        ),
        name="gram",
    )(order[:, 0], order[:, 1], *flat, *([so_far] if more else []))


def assemble_kernel(table, *refs):
    *groups, out = refs
    slot = 0
    for group in groups:
        for k in range(group.shape[0]):
            width = group.shape[2]
            at = pl.multiple_of(table[slot] * width, width)
            out[:, pl.ds(at, width)] = group[k]
            slot += 1


def assembled(table, groups, columns):
    return pl.pallas_call(
        assemble_kernel,
        in_specs=[pl.BlockSpec(memory_space=pltpu.SMEM)]
        + [pl.BlockSpec(memory_space=pltpu.VMEM)] * len(groups),
        out_specs=pl.BlockSpec(memory_space=pltpu.VMEM),
        out_shape=jax.ShapeDtypeStruct((groups[0].shape[1], columns), jnp.float32),
        cost_estimate=pl.CostEstimate(flops=0, bytes_accessed=1 << 20, transcendentals=0),
        name="assemble",
    )(table, *groups)


def together(*values):
    return lax.optimization_barrier(values)


def on_device(three_index, coefficients):
    rows, aux, width = three_index.shape
    by_aux = three_index.transpose(1, 0, 2)
    blk, col = lax.axis_index("blk"), lax.axis_index("col")
    place, zh = col // ZH, col % ZH
    swap_zh = [(x * ZH + 1 - h, x * ZH + h) for x in range(X) for h in range(ZH)]
    shares = lax.axis_size("col")

    def over_x(part):
        moved = lax.all_to_all(
            part, "col", split_axis=0, concat_axis=0, tiled=True, axis_index_groups=X_GROUPS
        )
        return moved.reshape(X, part.shape[0] // X, rows, width)

    def to_other_half(value):
        return lax.ppermute(value, "col", swap_zh)

    cut = aux - X
    ring = [coefficients.T]
    for step in range(1, X):
        route = [(((t + step) % X) * ZH + h, t * ZH + h) for t in range(X) for h in range(ZH)]
        ring.append(lax.ppermute(ring[0], "col", route))
    first, *ring = together(by_aux[:cut], *ring)
    ring = jnp.stack(ring)
    first_part = over_x(first)
    orbitals = lax.all_gather(ring, "blk", axis=0, tiled=False)
    last, first_part = together(by_aux[cut:], first_part)
    last_part = over_x(last)

    def sent(part, k):
        return to_other_half(transformed(part, k, orbitals, place, 1 - zh))

    def kept(part, k):
        return transformed(part, k, orbitals, place, zh)

    def neighbours(own):
        return fetched(own, other_core), fetched(own, next_row), fetched(own, previous_row)

    arrived_0, arrived_1 = sent(first_part, 0), sent(first_part, 1)
    own_0 = kept(first_part, 0) + arrived_0
    own_1 = kept(first_part, 1) + arrived_1
    other_0, below_0, above_0 = neighbours(own_0)
    arrived_2 = sent(last_part, 0)
    own_2 = kept(last_part, 0) + arrived_2
    other_0, below_0, above_0, own_1 = together(other_0, below_0, above_0, own_1)
    across_0 = fetched(below_0, over_to_across)
    other_1, below_1, above_1 = neighbours(own_1)
    other_1, below_1, above_1, across_0, own_2 = together(other_1, below_1, above_1, across_0, own_2)
    across_1 = fetched(below_1, over_to_across)
    other_2, below_2, above_2 = neighbours(own_2)
    known = [(own_0, own_1), (other_0, other_1), (below_0, below_1), (above_0, above_1)]
    early = gram(known, EARLY, shares)
    other_2, below_2, above_2, across_1, early = together(other_2, below_2, above_2, across_1, early)
    across_2 = fetched(below_2, over_to_across)
    known_2 = [(own_2,), (other_2,), (below_2,), (above_2,)]
    early = gram(known_2, EARLY, shares, early)
    late = gram(known + [(across_0, across_1)], LATE, shares)
    across_2, late = together(across_2, late)
    late = gram(known_2 + [(across_2,)], LATE, shares, late)

    def sent_home(tiles, pairs):
        summed = lax.all_to_all(tiles, "col", split_axis=0, concat_axis=0, tiled=True).sum(0)
        groups = []
        first = 0
        for row, target_of in enumerate(RELATED):
            count = sum(left == row for left, _ in pairs)
            if count:
                group = summed[first : first + count]
                groups.append(delivered(group, target_of) if row else group)
            first += count
        return groups

    groups = sent_home(early, EARLY) + sent_home(late, LATE)
    table = lax.dynamic_slice(jnp.asarray(column_table()), (blk, 0), (1, 16))[0]
    return assembled(table, groups, rows * lax.axis_size("blk"))


def solution(mesh):
    return jax.shard_map(
        on_device,
        mesh=mesh,
        in_specs=(P("blk", None, "col"), P("col", "blk")),
        out_specs=P(("blk", "col"), None),
        check_vma=False,
    )
```

```python
import functools

import jax
import jax.numpy as jnp
import numpy as np
from jax import lax
from jax.experimental import pallas as pl
from jax.experimental.pallas import tpu as pltpu
from jax.sharding import PartitionSpec as P

Y, ZL, CORES, X, ZH = 4, 2, 2, 4, 2
X_GROUPS = [[x * ZH + zh for x in range(X)] for zh in range(ZH)]
OWN, OTHER, BELOW, ABOVE, ACROSS = range(5)
EARLY = [(OWN, OWN), (OWN, OTHER), (OWN, BELOW), (OTHER, BELOW), (BELOW, ABOVE)]
LATE = [(OWN, ACROSS), (OTHER, ACROSS), (BELOW, ACROSS), (ABOVE, ACROSS)]
EARLY_ROUTES = [(OWN, [0, 1, 2], []), (OTHER, [3], []), (BELOW, [4], [2, 3]), (ABOVE, [], [4])]
LATE_ROUTES = [(OWN, [0], []), (OTHER, [1], []), (BELOW, [2], []), (ABOVE, [3], []),
               (ACROSS, [], [0, 1, 2, 3])]


def block_of(y, zl, core):
    return ((y % Y) * ZL + zl % ZL) * CORES + core % CORES


def upper(y):
    return (y % Y) // 2


def itself(y, zl, core):
    return y, zl, core


def other_core(y, zl, core):
    return y, zl, 1 - core


def next_row(y, zl, core):
    return y + 1, zl, core


def previous_row(y, zl, core):
    return y - 1, zl, (core + upper(y)) % 2


def next_across(y, zl, core):
    return y + 1, 1 - zl, (core + zl + upper(y)) % 2


def over_to_across(y, zl, core):
    return y, 1 - zl, (core + zl + upper(y)) % 2


RELATED = [itself, other_core, next_row, previous_row, next_across]


def places():
    return [(y, zl, core) for y in range(Y) for zl in range(ZL) for core in range(CORES)]


def fetched(value, source_of):
    route = [(block_of(*source_of(*at)), block_of(*at)) for at in places()]
    return lax.ppermute(value, "blk", route)


def delivered(value, target_of):
    route = [(block_of(*at), block_of(*target_of(*at))) for at in places()]
    return lax.ppermute(value, "blk", route)


def column_table():
    straight, turned = [], []
    for tiles, routes in ((EARLY, EARLY_ROUTES), (LATE, LATE_ROUTES)):
        for target, as_is, to_turn in routes:
            straight += [(target, tiles[k][1]) for k in as_is]
            turned += [(target, tiles[k][0]) for k in to_turn]
    table = np.zeros((len(places()), len(straight + turned)), np.int32)
    for slot, (target, column) in enumerate(straight + turned):
        for at in places():
            table[block_of(*RELATED[target](*at)), slot] = block_of(*RELATED[column](*at))
    return table


def high_and_low(value):
    high = value.astype(jnp.bfloat16)
    return high, (value - high.astype(jnp.float32)).astype(jnp.bfloat16)


def dot(left, right):
    return lax.dot_general(
        left, right, (((1,), (1,)), ((), ())), preferred_element_type=jnp.float32
    )


def transform_kernel(place, part, orbitals, out, high, low):
    width = part.shape[-1]

    @pl.when(pl.program_id(0) == 0)
    def _():
        for x in range(X):
            high[:, x * width : (x + 1) * width], low[:, x * width : (x + 1) * width] = (
                high_and_low(part[x, 0])
            )

    total = jnp.zeros(out.shape, jnp.float32)
    for x in range(X):
        slot = lax.rem(x - place[0] + X, X)
        block = orbitals[:, pl.ds(slot, 1)]
        c_high, c_low = high_and_low(block.reshape(out.shape[1], width))
        b_high = high[:, x * width : (x + 1) * width]
        b_low = low[:, x * width : (x + 1) * width]
        total += dot(b_high, c_high) + (dot(b_high, c_low) + dot(b_low, c_high))
    out[...] = total


def transformed(part, index, orbitals, place, half):
    rows, width = part.shape[2:]
    blocks, _, each, _ = orbitals.shape
    steps, run = 2, blocks // 4
    columns = run * each
    return pl.pallas_call(
        transform_kernel,
        grid_spec=pltpu.PrefetchScalarGridSpec(
            num_scalar_prefetch=1,
            grid=(steps,),
            in_specs=[
                pl.BlockSpec((X, 1, rows, width), lambda j, s: (0, index, 0, 0)),
                pl.BlockSpec((run, X, each, width), lambda j, s: (s[1] * 2 + j, 0, 0, 0)),
            ],
            out_specs=pl.BlockSpec((rows, columns), lambda j, s: (0, j)),
            scratch_shapes=[pltpu.VMEM((rows, X * width), jnp.bfloat16)] * 2,
        ),
        out_shape=jax.ShapeDtypeStruct((rows, steps * columns), jnp.float32),
        cost_estimate=pl.CostEstimate(
            flops=6 * rows * X * width * steps * columns, bytes_accessed=8 << 20, transcendentals=0
        ),
        name="transform",
    )(jnp.stack([place, half]), part, orbitals)


def gram_kernel(pairs, chunks, more, left_of, right_of, *refs):
    left_rows, right_rows = sides(pairs)
    count = (1 + max(left_rows + right_rows)) * chunks
    blocks, refs = refs[:count], refs[count:]
    if more:
        so_far, refs = refs[0], refs[1:]
    out, lefts, rights = refs
    depth = blocks[0].shape[1]
    for k, block in enumerate(blocks):
        high, low = high_and_low(block[...])
        row, first = k // chunks, k % chunks * 3
        for ref, rows, order in (
            (lefts, left_rows, (high, high, low)), (rights, right_rows, (high, low, high))
        ):
            if row in rows:
                for piece, value in enumerate(order, first):
                    ref[rows.index(row), :, piece * depth : (piece + 1) * depth] = value

    shares, tiles, part, width = out.shape

    @pl.loop(0, tiles)
    def _(t):
        tile = dot(lefts[left_of[t]], rights[right_of[t]]).reshape(shares, part, width)
        out[:, t] = so_far[:, t] + tile if more else tile


def sides(pairs):
    return sorted({left for left, _ in pairs}), sorted({right for _, right in pairs})


def gram(blocks, pairs, shares, so_far=None):
    rows, depth = blocks[0][0].shape
    chunks = len(blocks[0])
    flat = [chunk for block in blocks for chunk in block]
    tiles = len(pairs)
    more = so_far is not None
    left_rows, right_rows = sides(pairs)
    inputs = flat + ([so_far] if more else [])
    return pl.pallas_call(
        functools.partial(gram_kernel, pairs, chunks, more),
        in_specs=[pl.BlockSpec(memory_space=pltpu.SMEM)] * 2
        + [pl.BlockSpec(memory_space=pltpu.VMEM)] * len(inputs),
        out_specs=pl.BlockSpec(memory_space=pltpu.VMEM),
        scratch_shapes=[
            pltpu.VMEM((len(side), rows, 3 * chunks * depth), jnp.bfloat16)
            for side in (left_rows, right_rows)
        ],
        out_shape=jax.ShapeDtypeStruct((shares, tiles, rows // shares, rows), jnp.float32),
        cost_estimate=pl.CostEstimate(
            flops=6 * tiles * rows * rows * chunks * depth, bytes_accessed=6 << 20, transcendentals=0
        ),
        name="gram",
    )(
        np.array([left_rows.index(left) for left, _ in pairs], np.int32),
        np.array([right_rows.index(right) for _, right in pairs], np.int32),
        *inputs,
    )


def in_vmem(kernel, inputs, outputs, name, tables=()):
    return pl.pallas_call(
        kernel,
        in_specs=[pl.BlockSpec(memory_space=pltpu.SMEM)] * len(tables)
        + [pl.BlockSpec(memory_space=pltpu.VMEM)] * len(inputs),
        out_specs=[pl.BlockSpec(memory_space=pltpu.VMEM)] * len(outputs),
        out_shape=[jax.ShapeDtypeStruct(shape, jnp.float32) for shape in outputs],
        cost_estimate=pl.CostEstimate(flops=0, bytes_accessed=1 << 20, transcendentals=0),
        name=name,
    )(*tables, *inputs)


def summed(moved, routes):
    def kernel(moved_ref, *outs):
        for out, (_, as_is, to_turn) in zip(outs, routes):
            for k, tile in enumerate(as_is + to_turn):
                out[k] = moved_ref[:, tile].sum(0)

    shape = moved.shape[2:]
    outputs = [(len(as_is + to_turn),) + shape for _, as_is, to_turn in routes]
    return in_vmem(kernel, [moved], outputs, "sum")


def turned(slabs, picks, shares):
    part, width = slabs[0].shape[1:]

    def kernel(*refs):
        *ins, out = refs
        rows = [ref[k] for ref, ks in zip(ins, picks) for k in ks]
        rows += [jnp.zeros((part, width), jnp.float32)] * (width // part - len(rows))
        out[...] = jnp.concatenate(rows, axis=0).T.reshape(out.shape)

    return in_vmem(kernel, slabs, [(shares, width // shares, width)], "turn")[0]


def assembled(table, slabs, picks, crossed, columns):
    shares, part, width = crossed.shape

    def kernel(table_ref, *refs):
        *ins, crossed_ref, out = refs
        pieces = [ref[k] for ref, ks in zip(ins, picks) for k in ks]
        for k in range(columns // width - len(pieces)):
            lanes = slice(k * part, (k + 1) * part)
            pieces.append(jnp.concatenate([crossed_ref[s, :, lanes] for s in range(shares)], axis=1))
        for slot, piece in enumerate(pieces):
            out[:, pl.ds(pl.multiple_of(table_ref[slot] * width, width), width)] = piece

    return in_vmem(kernel, [*slabs, crossed], [(part, columns)], "assemble", [table])[0]


def together(*values):
    return lax.optimization_barrier(values)


def on_device(three_index, coefficients):
    rows, aux, width = three_index.shape
    by_aux = three_index.transpose(1, 0, 2)
    blk, col = lax.axis_index("blk"), lax.axis_index("col")
    place, zh = col // ZH, col % ZH
    swap_zh = [(x * ZH + 1 - h, x * ZH + h) for x in range(X) for h in range(ZH)]
    shares = lax.axis_size("col")

    def over_x(part):
        moved = lax.all_to_all(
            part, "col", split_axis=0, concat_axis=0, tiled=True, axis_index_groups=X_GROUPS
        )
        return moved.reshape(X, part.shape[0] // X, rows, width)

    def to_other_half(value):
        return lax.ppermute(value, "col", swap_zh)

    def over_col(tiles):
        return lax.all_to_all(tiles, "col", split_axis=0, concat_axis=0, tiled=True)

    cut = aux - X
    ring = [coefficients.T]
    for step in range(1, X):
        route = [(((t + step) % X) * ZH + h, t * ZH + h) for t in range(X) for h in range(ZH)]
        ring.append(lax.ppermute(ring[0], "col", route))
    first, *ring = together(by_aux[:cut], *ring)
    ring = jnp.stack(ring)
    first_part = over_x(first)
    orbitals = lax.all_gather(ring, "blk", axis=0, tiled=False)
    last, first_part = together(by_aux[cut:], first_part)
    last_part = over_x(last)

    def sent(part, k):
        return to_other_half(transformed(part, k, orbitals, place, 1 - zh))

    def kept(part, k):
        return transformed(part, k, orbitals, place, zh)

    def neighbours(own):
        return fetched(own, other_core), fetched(own, next_row), fetched(own, previous_row)

    arrived_0, arrived_1 = sent(first_part, 0), sent(first_part, 1)
    own_0 = kept(first_part, 0) + arrived_0
    own_1 = kept(first_part, 1) + arrived_1
    other_0, below_0, above_0 = neighbours(own_0)
    arrived_2 = sent(last_part, 0)
    own_2 = kept(last_part, 0) + arrived_2
    other_0, below_0, above_0, own_1 = together(other_0, below_0, above_0, own_1)
    across_0 = fetched(below_0, over_to_across)
    other_1, below_1, above_1 = neighbours(own_1)
    other_1, below_1, above_1, across_0, own_2 = together(other_1, below_1, above_1, across_0, own_2)
    across_1 = fetched(below_1, over_to_across)
    other_2, below_2, above_2 = neighbours(own_2)
    known = [(own_0, own_1), (other_0, other_1), (below_0, below_1), (above_0, above_1)]
    early = gram(known, EARLY, shares)
    other_2, below_2, above_2, across_1, early = together(other_2, below_2, above_2, across_1, early)
    across_2 = fetched(below_2, over_to_across)
    known_2 = [(own_2,), (other_2,), (below_2,), (above_2,)]
    early = gram(known_2, EARLY, shares, early)
    late = gram(known + [(across_0, across_1)], LATE, shares)
    across_2, late, early_moved = together(across_2, late, over_col(early))
    late = gram(known_2 + [(across_2,)], LATE, shares, late)

    def sent_home(moved, routes):
        groups = summed(moved, routes)
        return [
            delivered(group, RELATED[target]) if target else group
            for group, (target, _, _) in zip(groups, routes)
        ]

    late_moved, *early_slabs = together(over_col(late), *sent_home(early_moved, EARLY_ROUTES))
    slabs = early_slabs + sent_home(late_moved, LATE_ROUTES)
    routes = EARLY_ROUTES + LATE_ROUTES
    straight = [range(len(as_is)) for _, as_is, _ in routes]
    to_turn = [range(len(as_is), len(as_is + to_turn)) for _, as_is, to_turn in routes]

    def chosen(picks):
        return [slab for slab, ks in zip(slabs, picks) if len(ks)], [ks for ks in picks if len(ks)]

    crossed = over_col(turned(*chosen(to_turn), shares))
    table = lax.dynamic_slice(jnp.asarray(column_table()), (blk, 0), (1, 16))[0]
    return assembled(table, *chosen(straight), crossed, rows * lax.axis_size("blk"))


def solution(mesh):
    return jax.shard_map(
        on_device,
        mesh=mesh,
        in_specs=(P("blk", None, "col"), P("col", "blk")),
        out_specs=P(("blk", "col"), None),
        check_vma=False,
    )
```

```python
import functools

import jax
import jax.numpy as jnp
import numpy as np
from jax import lax
from jax.experimental import pallas as pl
from jax.experimental.pallas import tpu as pltpu
from jax.sharding import PartitionSpec as P

Y, ZL, CORES, X, ZH = 4, 2, 2, 4, 2
X_GROUPS = [[x * ZH + zh for x in range(X)] for zh in range(ZH)]
OWN, OTHER, BELOW, ABOVE, ACROSS = range(5)
EARLY = [(OWN, OWN), (OWN, OTHER), (OWN, BELOW), (OTHER, BELOW), (BELOW, ABOVE)]
LATE = [(OWN, ACROSS), (OTHER, ACROSS), (BELOW, ACROSS), (ABOVE, ACROSS)]
ROUTES = [(OWN, [0, 1, 2, 5], []), (OTHER, [3, 6], []), (BELOW, [4, 7], [2, 3]), (ABOVE, [8], [4]),
          (ACROSS, [], [5, 6, 7, 8])]


def block_of(y, zl, core):
    return ((y % Y) * ZL + zl % ZL) * CORES + core % CORES


def upper(y):
    return (y % Y) // 2


def itself(y, zl, core):
    return y, zl, core


def other_core(y, zl, core):
    return y, zl, 1 - core


def next_row(y, zl, core):
    return y + 1, zl, core


def previous_row(y, zl, core):
    return y - 1, zl, (core + upper(y)) % 2


def next_across(y, zl, core):
    return y + 1, 1 - zl, (core + zl + upper(y)) % 2


def over_to_across(y, zl, core):
    return y, 1 - zl, (core + zl + upper(y)) % 2


RELATED = [itself, other_core, next_row, previous_row, next_across]


def places():
    return [(y, zl, core) for y in range(Y) for zl in range(ZL) for core in range(CORES)]


def fetched(value, source_of):
    route = [(block_of(*source_of(*at)), block_of(*at)) for at in places()]
    return lax.ppermute(value, "blk", route)


def delivered(value, target_of):
    route = [(block_of(*at), block_of(*target_of(*at))) for at in places()]
    return lax.ppermute(value, "blk", route)


def column_table():
    tiles = EARLY + LATE
    straight = [(target, tiles[k][1]) for target, as_is, _ in ROUTES for k in as_is]
    turned = [(target, tiles[k][0]) for target, _, to_turn in ROUTES for k in to_turn]
    table = np.zeros((len(places()), len(straight + turned)), np.int32)
    for slot, (target, column) in enumerate(straight + turned):
        for at in places():
            table[block_of(*RELATED[target](*at)), slot] = block_of(*RELATED[column](*at))
    return table


def high_and_low(value):
    high = value.astype(jnp.bfloat16)
    return high, (value - high.astype(jnp.float32)).astype(jnp.bfloat16)


def dot(left, right):
    return lax.dot_general(
        left, right, (((1,), (1,)), ((), ())), preferred_element_type=jnp.float32
    )


def transform_kernel(place, part, orbitals, out, high, low):
    width = part.shape[-1]

    @pl.when(pl.program_id(0) == 0)
    def _():
        for x in range(X):
            high[:, x * width : (x + 1) * width], low[:, x * width : (x + 1) * width] = (
                high_and_low(part[x, 0])
            )

    total = jnp.zeros(out.shape, jnp.float32)
    for x in range(X):
        slot = lax.rem(x - place[0] + X, X)
        block = orbitals[:, pl.ds(slot, 1)]
        c_high, c_low = high_and_low(block.reshape(out.shape[1], width))
        b_high = high[:, x * width : (x + 1) * width]
        b_low = low[:, x * width : (x + 1) * width]
        total += dot(b_high, c_high) + (dot(b_high, c_low) + dot(b_low, c_high))
    out[...] = total


def transformed(part, index, orbitals, place, half):
    rows, width = part.shape[2:]
    blocks, _, each, _ = orbitals.shape
    steps, run = 2, blocks // 4
    columns = run * each
    return pl.pallas_call(
        transform_kernel,
        grid_spec=pltpu.PrefetchScalarGridSpec(
            num_scalar_prefetch=1,
            grid=(steps,),
            in_specs=[
                pl.BlockSpec((X, 1, rows, width), lambda j, s: (0, index, 0, 0)),
                pl.BlockSpec((run, X, each, width), lambda j, s: (s[1] * 2 + j, 0, 0, 0)),
            ],
            out_specs=pl.BlockSpec((rows, columns), lambda j, s: (0, j)),
            scratch_shapes=[pltpu.VMEM((rows, X * width), jnp.bfloat16)] * 2,
        ),
        out_shape=jax.ShapeDtypeStruct((rows, steps * columns), jnp.float32),
        cost_estimate=pl.CostEstimate(
            flops=0, bytes_accessed=0, transcendentals=0
        ),
        name="transform",
    )(jnp.stack([place, half]), part, orbitals)


def gram_kernel(pairs, chunks, more, ahead, left_of, right_of, *refs):
    left_rows, right_rows = sides(pairs)
    count = (1 + max(left_rows + right_rows)) * chunks
    blocks, refs = refs[:count], refs[count:]
    if more:
        so_far, refs = refs[0], refs[1:]
    if ahead:
        before, refs = refs[0], refs[1:]
    out, lefts, rights = refs
    depth = blocks[0].shape[1]
    for k, block in enumerate(blocks):
        high, low = high_and_low(block[...])
        row, first = k // chunks, k % chunks * 3
        for ref, rows, order in (
            (lefts, left_rows, (high, high, low)), (rights, right_rows, (high, low, high))
        ):
            if row in rows:
                for piece, value in enumerate(order, first):
                    ref[rows.index(row), :, piece * depth : (piece + 1) * depth] = value

    shares, _, part, width = out.shape
    if ahead:
        out[:, :ahead] = before[...]

    @pl.loop(0, len(pairs))
    def _(t):
        tile = dot(lefts[left_of[t]], rights[right_of[t]]).reshape(shares, part, width)
        out[:, ahead + t] = so_far[:, t] + tile if more else tile


def sides(pairs):
    return sorted({left for left, _ in pairs}), sorted({right for _, right in pairs})


def gram(blocks, pairs, shares, so_far=None, before=None):
    rows, depth = blocks[0][0].shape
    chunks = len(blocks[0])
    flat = [chunk for block in blocks for chunk in block]
    more = so_far is not None
    ahead = 0 if before is None else before.shape[1]
    tiles = ahead + len(pairs)
    left_rows, right_rows = sides(pairs)
    inputs = flat + ([so_far] if more else []) + ([before] if ahead else [])
    return pl.pallas_call(
        functools.partial(gram_kernel, pairs, chunks, more, ahead),
        in_specs=[pl.BlockSpec(memory_space=pltpu.SMEM)] * 2
        + [pl.BlockSpec(memory_space=pltpu.VMEM)] * len(inputs),
        out_specs=pl.BlockSpec(memory_space=pltpu.VMEM),
        scratch_shapes=[
            pltpu.VMEM((len(side), rows, 3 * chunks * depth), jnp.bfloat16)
            for side in (left_rows, right_rows)
        ],
        out_shape=jax.ShapeDtypeStruct((shares, tiles, rows // shares, rows), jnp.float32),
        cost_estimate=pl.CostEstimate(
            flops=0, bytes_accessed=0, transcendentals=0
        ),
        name="gram",
    )(
        np.array([left_rows.index(left) for left, _ in pairs], np.int32),
        np.array([right_rows.index(right) for _, right in pairs], np.int32),
        *inputs,
    )


def in_vmem(kernel, inputs, outputs, name, tables=()):
    return pl.pallas_call(
        kernel,
        in_specs=[pl.BlockSpec(memory_space=pltpu.SMEM)] * len(tables)
        + [pl.BlockSpec(memory_space=pltpu.VMEM)] * len(inputs),
        out_specs=[pl.BlockSpec(memory_space=pltpu.VMEM)] * len(outputs),
        out_shape=[jax.ShapeDtypeStruct(shape, jnp.float32) for shape in outputs],
        cost_estimate=pl.CostEstimate(flops=0, bytes_accessed=1 << 20, transcendentals=0),
        name=name,
    )(*tables, *inputs)


def summed(moved):
    def kernel(moved_ref, *outs):
        for out, (_, as_is, to_turn) in zip(outs, ROUTES):
            for k, tile in enumerate(as_is + to_turn):
                out[k] = moved_ref[:, tile].sum(0)

    shape = moved.shape[2:]
    outputs = [(len(as_is + to_turn),) + shape for _, as_is, to_turn in ROUTES]
    return in_vmem(kernel, [moved], outputs, "sum")


def turned(slabs, picks, shares):
    part, width = slabs[0].shape[1:]

    def kernel(*refs):
        *ins, out = refs
        rows = [ref[k] for ref, ks in zip(ins, picks) for k in ks]
        rows += [jnp.zeros((part, width), jnp.float32)] * (width // part - len(rows))
        out[...] = jnp.concatenate(rows, axis=0).T.reshape(out.shape)

    return in_vmem(kernel, slabs, [(shares, width // shares, width)], "turn")[0]


def assembled(table, slabs, picks, crossed, columns):
    shares, part, width = crossed.shape

    def kernel(table_ref, *refs):
        *ins, crossed_ref, out = refs
        pieces = [ref[k] for ref, ks in zip(ins, picks) for k in ks]
        for k in range(columns // width - len(pieces)):
            lanes = slice(k * part, (k + 1) * part)
            pieces.append(jnp.concatenate([crossed_ref[s, :, lanes] for s in range(shares)], axis=1))
        for slot, piece in enumerate(pieces):
            out[:, pl.ds(pl.multiple_of(table_ref[slot] * width, width), width)] = piece

    return in_vmem(kernel, [*slabs, crossed], [(part, columns)], "assemble", [table])[0]


def together(*values):
    return lax.optimization_barrier(values)


def on_device(three_index, coefficients):
    rows, aux, width = three_index.shape
    by_aux = three_index.transpose(1, 0, 2)
    blk, col = lax.axis_index("blk"), lax.axis_index("col")
    place, zh = col // ZH, col % ZH
    swap_zh = [(x * ZH + 1 - h, x * ZH + h) for x in range(X) for h in range(ZH)]
    shares = lax.axis_size("col")

    def over_x(part):
        moved = lax.all_to_all(
            part, "col", split_axis=0, concat_axis=0, tiled=True, axis_index_groups=X_GROUPS
        )
        return moved.reshape(X, part.shape[0] // X, rows, width)

    def to_other_half(value):
        return lax.ppermute(value, "col", swap_zh)

    def over_col(tiles):
        return lax.all_to_all(tiles, "col", split_axis=0, concat_axis=0, tiled=True)

    cut = aux - X
    ring = [coefficients.T]
    for step in range(1, X):
        route = [(((t + step) % X) * ZH + h, t * ZH + h) for t in range(X) for h in range(ZH)]
        ring.append(lax.ppermute(ring[0], "col", route))
    first, *ring = together(by_aux[:cut], *ring)
    ring = jnp.stack(ring)
    first_part = over_x(first)
    orbitals = lax.all_gather(ring, "blk", axis=0, tiled=False)
    last, first_part = together(by_aux[cut:], first_part)
    last_part = over_x(last)

    def sent(part, k):
        return to_other_half(transformed(part, k, orbitals, place, 1 - zh))

    def kept(part, k):
        return transformed(part, k, orbitals, place, zh)

    def neighbours(own):
        return fetched(own, other_core), fetched(own, next_row), fetched(own, previous_row)

    arrived_0, arrived_1 = sent(first_part, 0), sent(first_part, 1)
    own_0 = kept(first_part, 0) + arrived_0
    own_1 = kept(first_part, 1) + arrived_1
    own_1, last_part = together(own_1, last_part)
    other_0, below_0, above_0 = neighbours(own_0)
    arrived_2 = sent(last_part, 0)
    own_2 = kept(last_part, 0) + arrived_2
    other_0, below_0, above_0, own_1 = together(other_0, below_0, above_0, own_1)
    across_0 = fetched(below_0, over_to_across)
    other_1, below_1, above_1 = neighbours(own_1)
    other_1, below_1, above_1, across_0, own_2 = together(other_1, below_1, above_1, across_0, own_2)
    across_1 = fetched(below_1, over_to_across)
    other_2, below_2, above_2 = neighbours(own_2)
    known = [(own_0, own_1), (other_0, other_1), (below_0, below_1), (above_0, above_1)]
    early = gram(known, EARLY, shares)
    other_2, below_2, above_2, across_1, early = together(other_2, below_2, above_2, across_1, early)
    across_2 = fetched(below_2, over_to_across)
    known_2 = [(own_2,), (other_2,), (below_2,), (above_2,)]
    early = gram(known_2, EARLY, shares, early)
    late = gram(known + [(across_0, across_1)], LATE, shares)
    across_2, late, early = together(across_2, late, early)
    tiles = gram(known_2 + [(across_2,)], LATE, shares, late, early)

    slabs = [
        delivered(slab, RELATED[target]) if target else slab
        for slab, (target, _, _) in zip(summed(over_col(tiles)), ROUTES)
    ]
    straight = [range(len(as_is)) for _, as_is, _ in ROUTES]
    to_turn = [range(len(as_is), len(as_is + to_turn)) for _, as_is, to_turn in ROUTES]

    def chosen(picks):
        return [slab for slab, ks in zip(slabs, picks) if len(ks)], [ks for ks in picks if len(ks)]

    crossed = over_col(turned(*chosen(to_turn), shares))
    table = lax.dynamic_slice(jnp.asarray(column_table()), (blk, 0), (1, 16))[0]
    return assembled(table, *chosen(straight), crossed, rows * lax.axis_size("blk"))


def solution(mesh):
    return jax.shard_map(
        on_device,
        mesh=mesh,
        in_specs=(P("blk", None, "col"), P("col", "blk")),
        out_specs=P(("blk", "col"), None),
        check_vma=False,
    )
```

```python
import functools

import jax
import jax.numpy as jnp
import numpy as np
from jax import lax
from jax.experimental import pallas as pl
from jax.experimental.pallas import tpu as pltpu
from jax.sharding import PartitionSpec as P

Y, ZL, CORES, X, ZH = 4, 2, 2, 4, 2
X_GROUPS = [[x * ZH + zh for x in range(X)] for zh in range(ZH)]
OWN, OTHER, BELOW, ABOVE, ACROSS = range(5)
EARLY = [(OWN, OWN), (OWN, OTHER), (OWN, BELOW), (OTHER, BELOW), (BELOW, ABOVE)]
LATE = [(OWN, ACROSS), (OTHER, ACROSS), (BELOW, ACROSS), (ABOVE, ACROSS)]
ROUTES = [(OWN, [0, 1, 2, 5], []), (OTHER, [3, 6], []), (BELOW, [4, 7], [2, 3]), (ABOVE, [8], [4]),
          (ACROSS, [], [5, 6, 7, 8])]


def block_of(y, zl, core):
    return ((y % Y) * ZL + zl % ZL) * CORES + core % CORES


def upper(y):
    return (y % Y) // 2


def itself(y, zl, core):
    return y, zl, core


def other_core(y, zl, core):
    return y, zl, 1 - core


def next_row(y, zl, core):
    return y + 1, zl, core


def previous_row(y, zl, core):
    return y - 1, zl, (core + upper(y)) % 2


def next_across(y, zl, core):
    return y + 1, 1 - zl, (core + zl + upper(y)) % 2


def over_to_across(y, zl, core):
    return y, 1 - zl, (core + zl + upper(y)) % 2


RELATED = [itself, other_core, next_row, previous_row, next_across]


def places():
    return [(y, zl, core) for y in range(Y) for zl in range(ZL) for core in range(CORES)]


def fetched(value, source_of):
    route = [(block_of(*source_of(*at)), block_of(*at)) for at in places()]
    return lax.ppermute(value, "blk", route)


def delivered(value, target_of):
    route = [(block_of(*at), block_of(*target_of(*at))) for at in places()]
    return lax.ppermute(value, "blk", route)


def column_table():
    tiles = EARLY + LATE
    straight = [(target, tiles[k][1]) for target, as_is, _ in ROUTES for k in as_is]
    turned = [(target, tiles[k][0]) for target, _, to_turn in ROUTES for k in to_turn]
    table = np.zeros((len(places()), len(straight + turned)), np.int32)
    for slot, (target, column) in enumerate(straight + turned):
        for at in places():
            table[block_of(*RELATED[target](*at)), slot] = block_of(*RELATED[column](*at))
    return table


def high_and_low(value):
    high = value.astype(jnp.bfloat16)
    return high, (value - high.astype(jnp.float32)).astype(jnp.bfloat16)


def dot(left, right):
    return lax.dot_general(
        left, right, (((1,), (1,)), ((), ())), preferred_element_type=jnp.float32
    )


def transform_kernel(index, scalars, part, orbitals, out, rows_in, orbitals_in, sems):
    place, half = scalars[0], scalars[1]
    run, each, width = orbitals_in.shape[1:]
    copies = []
    for k in range(X):
        x = lax.rem(place + k, X)
        copies.append((
            pltpu.make_async_copy(part.at[x, index], rows_in.at[k], sems.at[0, k]),
            pltpu.make_async_copy(
                orbitals.at[pl.ds(half * run, run), k], orbitals_in.at[k], sems.at[1, k]
            ),
        ))
    for of_rows, of_orbitals in copies:
        of_rows.start()
        of_orbitals.start()
    for k, (of_rows, of_orbitals) in enumerate(copies):
        of_rows.wait()
        of_orbitals.wait()
        b_high, b_low = high_and_low(rows_in[k])
        c_high, c_low = high_and_low(orbitals_in[k].reshape(run * each, width))
        term = dot(b_high, c_high) + (dot(b_high, c_low) + dot(b_low, c_high))
        out[...] = out[...] + term if k else term


def transformed(part, index, orbitals, place, half):
    rows, width = part.shape[2:]
    blocks, _, each, _ = orbitals.shape
    run = blocks // ZH
    return pl.pallas_call(
        functools.partial(transform_kernel, index),
        in_specs=[pl.BlockSpec(memory_space=pltpu.SMEM)] + [pl.BlockSpec(memory_space=pl.ANY)] * 2,
        out_specs=pl.BlockSpec(memory_space=pltpu.VMEM),
        out_shape=jax.ShapeDtypeStruct((rows, run * each), jnp.float32),
        scratch_shapes=[
            pltpu.VMEM((X, rows, width), jnp.float32),
            pltpu.VMEM((X, run, each, width), jnp.float32),
            pltpu.SemaphoreType.DMA((2, X)),
        ],
        cost_estimate=pl.CostEstimate(flops=0, bytes_accessed=0, transcendentals=0),
        name="transform",
    )(jnp.stack([place, half]), part, orbitals)


def gram_kernel(pairs, chunks, more, ahead, *refs):
    left_rows, right_rows = sides(pairs)
    count = (1 + max(left_rows + right_rows)) * chunks
    blocks, refs = refs[:count], refs[count:]
    if more:
        so_far, refs = refs[0], refs[1:]
    if ahead:
        before, refs = refs[0], refs[1:]
    out, lefts, rights = refs
    depth = blocks[0].shape[1]
    for k, block in enumerate(blocks):
        high, low = high_and_low(block[...])
        row, first = k // chunks, k % chunks * 3
        for ref, rows, order in (
            (lefts, left_rows, (high, high, low)), (rights, right_rows, (high, low, high))
        ):
            if row in rows:
                for piece, value in enumerate(order, first):
                    ref[rows.index(row), :, piece * depth : (piece + 1) * depth] = value

    shares, _, part, width = out.shape
    if ahead:
        out[:, :ahead] = before[...]

    for t, (left, right) in enumerate(pairs):
        tile = dot(lefts[left_rows.index(left)], rights[right_rows.index(right)])
        tile = tile.reshape(shares, part, width)
        out[:, ahead + t] = so_far[:, t] + tile if more else tile


def sides(pairs):
    return sorted({left for left, _ in pairs}), sorted({right for _, right in pairs})


def gram(blocks, pairs, shares, so_far=None, before=None):
    rows, depth = blocks[0][0].shape
    chunks = len(blocks[0])
    flat = [chunk for block in blocks for chunk in block]
    more = so_far is not None
    ahead = 0 if before is None else before.shape[1]
    tiles = ahead + len(pairs)
    left_rows, right_rows = sides(pairs)
    inputs = flat + ([so_far] if more else []) + ([before] if ahead else [])
    return pl.pallas_call(
        functools.partial(gram_kernel, pairs, chunks, more, ahead),
        in_specs=[pl.BlockSpec(memory_space=pltpu.VMEM)] * len(inputs),
        out_specs=pl.BlockSpec(memory_space=pltpu.VMEM),
        scratch_shapes=[
            pltpu.VMEM((len(side), rows, 3 * chunks * depth), jnp.bfloat16)
            for side in (left_rows, right_rows)
        ],
        out_shape=jax.ShapeDtypeStruct((shares, tiles, rows // shares, rows), jnp.float32),
        cost_estimate=pl.CostEstimate(
            flops=0, bytes_accessed=0, transcendentals=0
        ),
        name="gram",
    )(*inputs)


def in_vmem(kernel, inputs, outputs, name, tables=()):
    return pl.pallas_call(
        kernel,
        in_specs=[pl.BlockSpec(memory_space=pltpu.SMEM)] * len(tables)
        + [pl.BlockSpec(memory_space=pltpu.VMEM)] * len(inputs),
        out_specs=[pl.BlockSpec(memory_space=pltpu.VMEM)] * len(outputs),
        out_shape=[jax.ShapeDtypeStruct(shape, jnp.float32) for shape in outputs],
        cost_estimate=pl.CostEstimate(flops=0, bytes_accessed=1 << 20, transcendentals=0),
        name=name,
    )(*tables, *inputs)


def summed(moved):
    def kernel(moved_ref, *outs):
        for out, (_, as_is, to_turn) in zip(outs, ROUTES):
            for k, tile in enumerate(as_is + to_turn):
                out[k] = moved_ref[:, tile].sum(0)

    shape = moved.shape[2:]
    outputs = [(len(as_is + to_turn),) + shape for _, as_is, to_turn in ROUTES]
    return in_vmem(kernel, [moved], outputs, "sum")


def turned(slabs, picks, shares):
    part, width = slabs[0].shape[1:]

    def kernel(*refs):
        *ins, out = refs
        rows = [ref[k] for ref, ks in zip(ins, picks) for k in ks]
        rows += [jnp.zeros((part, width), jnp.float32)] * (width // part - len(rows))
        out[...] = jnp.concatenate(rows, axis=0).T.reshape(out.shape)

    return in_vmem(kernel, slabs, [(shares, width // shares, width)], "turn")[0]


def assembled(table, slabs, picks, crossed, columns):
    shares, part, width = crossed.shape

    def kernel(table_ref, *refs):
        *ins, crossed_ref, out = refs
        pieces = [ref[k] for ref, ks in zip(ins, picks) for k in ks]
        for k in range(columns // width - len(pieces)):
            lanes = slice(k * part, (k + 1) * part)
            pieces.append(jnp.concatenate([crossed_ref[s, :, lanes] for s in range(shares)], axis=1))
        for slot, piece in enumerate(pieces):
            out[:, pl.ds(pl.multiple_of(table_ref[slot] * width, width), width)] = piece

    return in_vmem(kernel, [*slabs, crossed], [(part, columns)], "assemble", [table])[0]


def together(*values):
    return lax.optimization_barrier(values)


def on_device(three_index, coefficients):
    rows, aux, width = three_index.shape
    by_aux = three_index.transpose(1, 0, 2)
    blk, col = lax.axis_index("blk"), lax.axis_index("col")
    place, zh = col // ZH, col % ZH
    swap_zh = [(x * ZH + 1 - h, x * ZH + h) for x in range(X) for h in range(ZH)]
    shares = lax.axis_size("col")

    def over_x(part):
        moved = lax.all_to_all(
            part, "col", split_axis=0, concat_axis=0, tiled=True, axis_index_groups=X_GROUPS
        )
        return moved.reshape(X, part.shape[0] // X, rows, width)

    def to_other_half(value):
        return lax.ppermute(value, "col", swap_zh)

    def over_col(tiles):
        return lax.all_to_all(tiles, "col", split_axis=0, concat_axis=0, tiled=True)

    cut = aux - X
    ring = [coefficients.T]
    for step in range(1, X):
        route = [(((t + step) % X) * ZH + h, t * ZH + h) for t in range(X) for h in range(ZH)]
        ring.append(lax.ppermute(ring[0], "col", route))
    first, *ring = together(by_aux[:cut], *ring)
    ring = jnp.stack(ring)
    first_part = over_x(first)
    orbitals = lax.all_gather(ring, "blk", axis=0, tiled=False)
    last, first_part = together(by_aux[cut:], first_part)
    last_part = over_x(last)

    def to_send(part, k):
        return transformed(part, k, orbitals, place, 1 - zh)

    def kept(part, k):
        return transformed(part, k, orbitals, place, zh)

    def neighbours(own):
        return fetched(own, other_core), fetched(own, next_row), fetched(own, previous_row)

    arrived_0 = to_other_half(to_send(first_part, 0))
    arrived_1 = to_other_half(to_send(first_part, 1))
    own_0 = kept(first_part, 0) + arrived_0
    other_0, below_0, above_0 = neighbours(own_0)
    leaving_2, first_part = together(to_send(last_part, 0), first_part)
    arrived_2 = to_other_half(leaving_2)
    own_1 = kept(first_part, 1) + arrived_1
    own_2 = kept(last_part, 0) + arrived_2
    other_0, below_0, above_0, own_1 = together(other_0, below_0, above_0, own_1)
    across_0 = fetched(below_0, over_to_across)
    other_1, below_1, above_1 = neighbours(own_1)
    other_1, below_1, above_1, across_0, own_2 = together(other_1, below_1, above_1, across_0, own_2)
    across_1 = fetched(below_1, over_to_across)
    other_2, below_2, above_2 = neighbours(own_2)
    known = [(own_0, own_1), (other_0, other_1), (below_0, below_1), (above_0, above_1)]
    early = gram(known, EARLY, shares)
    other_2, below_2, above_2, across_1, early = together(other_2, below_2, above_2, across_1, early)
    across_2 = fetched(below_2, over_to_across)
    known_2 = [(own_2,), (other_2,), (below_2,), (above_2,)]
    early = gram(known_2, EARLY, shares, early)
    late = gram(known + [(across_0, across_1)], LATE, shares)
    across_2, late, early = together(across_2, late, early)
    tiles = gram(known_2 + [(across_2,)], LATE, shares, late, early)

    slabs = [
        delivered(slab, RELATED[target]) if target else slab
        for slab, (target, _, _) in zip(summed(over_col(tiles)), ROUTES)
    ]
    straight = [range(len(as_is)) for _, as_is, _ in ROUTES]
    to_turn = [range(len(as_is), len(as_is + to_turn)) for _, as_is, to_turn in ROUTES]

    def chosen(picks):
        return [slab for slab, ks in zip(slabs, picks) if len(ks)], [ks for ks in picks if len(ks)]

    crossed = over_col(turned(*chosen(to_turn), shares))
    table = lax.dynamic_slice(jnp.asarray(column_table()), (blk, 0), (1, 16))[0]
    return assembled(table, *chosen(straight), crossed, rows * lax.axis_size("blk"))


def solution(mesh):
    return jax.shard_map(
        on_device,
        mesh=mesh,
        in_specs=(P("blk", None, "col"), P("col", "blk")),
        out_specs=P(("blk", "col"), None),
        check_vma=False,
    )
```

```python
import functools

import jax
import jax.numpy as jnp
import numpy as np
from jax import lax
from jax.experimental import pallas as pl
from jax.experimental.pallas import tpu as pltpu
from jax.sharding import PartitionSpec as P

Y, ZL, CORES, X, ZH = 4, 2, 2, 4, 2
X_GROUPS = [[x * ZH + zh for x in range(X)] for zh in range(ZH)]
OWN, OTHER, BELOW, ABOVE, ACROSS = range(5)
EARLY = [(OWN, OWN), (OWN, OTHER), (OWN, BELOW), (OTHER, BELOW), (BELOW, ABOVE)]
LATE = [(OWN, ACROSS), (OTHER, ACROSS), (BELOW, ACROSS), (ABOVE, ACROSS)]
EARLY_ROUTES = [(OWN, [0, 1, 2], []), (OTHER, [3], []), (BELOW, [4], [2, 3]), (ABOVE, [], [4])]
LATE_ROUTES = [(OWN, [0], []), (OTHER, [1], []), (BELOW, [2], []), (ABOVE, [3], []),
               (ACROSS, [], [0, 1, 2, 3])]
ROUTES = EARLY_ROUTES + LATE_ROUTES
LATE_COST = 20_000_000_000


def block_of(y, zl, core):
    return ((y % Y) * ZL + zl % ZL) * CORES + core % CORES


def upper(y):
    return (y % Y) // 2


def itself(y, zl, core):
    return y, zl, core


def other_core(y, zl, core):
    return y, zl, 1 - core


def next_row(y, zl, core):
    return y + 1, zl, core


def previous_row(y, zl, core):
    return y - 1, zl, (core + upper(y)) % 2


def next_across(y, zl, core):
    return y + 1, 1 - zl, (core + zl + upper(y)) % 2


def over_to_across(y, zl, core):
    return y, 1 - zl, (core + zl + upper(y)) % 2


RELATED = [itself, other_core, next_row, previous_row, next_across]


def places():
    return [(y, zl, core) for y in range(Y) for zl in range(ZL) for core in range(CORES)]


def fetched(value, source_of):
    route = [(block_of(*source_of(*at)), block_of(*at)) for at in places()]
    return lax.ppermute(value, "blk", route)


def delivered(value, target_of):
    route = [(block_of(*at), block_of(*target_of(*at))) for at in places()]
    return lax.ppermute(value, "blk", route)


def column_table():
    straight, turned = [], []
    for tiles, routes in ((EARLY, EARLY_ROUTES), (LATE, LATE_ROUTES)):
        for target, as_is, to_turn in routes:
            straight += [(target, tiles[k][1]) for k in as_is]
            turned += [(target, tiles[k][0]) for k in to_turn]
    table = np.zeros((len(places()), len(straight + turned)), np.int32)
    for slot, (target, column) in enumerate(straight + turned):
        for at in places():
            table[block_of(*RELATED[target](*at)), slot] = block_of(*RELATED[column](*at))
    return table


def high_and_low(value):
    high = value.astype(jnp.bfloat16)
    return high, (value - high.astype(jnp.float32)).astype(jnp.bfloat16)


def dot(left, right):
    return lax.dot_general(
        left, right, (((1,), (1,)), ((), ())), preferred_element_type=jnp.float32
    )


def transform_kernel(index, scalars, part, orbitals, out, rows_in, orbitals_in, sems):
    place, half = scalars[0], scalars[1]
    run, each, width = orbitals_in.shape[1:]
    copies = []
    for k in range(X):
        x = lax.rem(place + k, X)
        copies.append((
            pltpu.make_async_copy(part.at[x, index], rows_in.at[k], sems.at[0, k]),
            pltpu.make_async_copy(
                orbitals.at[pl.ds(half * run, run), k], orbitals_in.at[k], sems.at[1, k]
            ),
        ))
    for of_rows, of_orbitals in copies:
        of_rows.start()
        of_orbitals.start()
    for k, (of_rows, of_orbitals) in enumerate(copies):
        of_rows.wait()
        of_orbitals.wait()
        b_high, b_low = high_and_low(rows_in[k])
        c_high, c_low = high_and_low(orbitals_in[k].reshape(run * each, width))
        term = dot(b_high, c_high) + (dot(b_high, c_low) + dot(b_low, c_high))
        out[...] = out[...] + term if k else term


def transformed(part, index, orbitals, place, half):
    rows, width = part.shape[2:]
    blocks, _, each, _ = orbitals.shape
    run = blocks // ZH
    return pl.pallas_call(
        functools.partial(transform_kernel, index),
        in_specs=[pl.BlockSpec(memory_space=pltpu.SMEM)] + [pl.BlockSpec(memory_space=pl.ANY)] * 2,
        out_specs=pl.BlockSpec(memory_space=pltpu.VMEM),
        out_shape=jax.ShapeDtypeStruct((rows, run * each), jnp.float32),
        scratch_shapes=[
            pltpu.VMEM((X, rows, width), jnp.float32),
            pltpu.VMEM((X, run, each, width), jnp.float32),
            pltpu.SemaphoreType.DMA((2, X)),
        ],
        cost_estimate=pl.CostEstimate(flops=0, bytes_accessed=0, transcendentals=0),
        name="transform",
    )(jnp.stack([place, half]), part, orbitals)


def gram_kernel(pairs, chunks, more, *refs):
    left_rows, right_rows = sides(pairs)
    count = (1 + max(left_rows + right_rows)) * chunks
    blocks, refs = refs[:count], refs[count:]
    if more:
        so_far, refs = refs[0], refs[1:]
    out, lefts, rights = refs
    depth = blocks[0].shape[1]
    for k, block in enumerate(blocks):
        high, low = high_and_low(block[...])
        row, first = k // chunks, k % chunks * 3
        for ref, rows, order in (
            (lefts, left_rows, (high, high, low)), (rights, right_rows, (high, low, high))
        ):
            if row in rows:
                for piece, value in enumerate(order, first):
                    ref[rows.index(row), :, piece * depth : (piece + 1) * depth] = value

    shares, _, part, width = out.shape
    for t, (left, right) in enumerate(pairs):
        tile = dot(lefts[left_rows.index(left)], rights[right_rows.index(right)])
        tile = tile.reshape(shares, part, width)
        out[:, t] = so_far[:, t] + tile if more else tile


def sides(pairs):
    return sorted({left for left, _ in pairs}), sorted({right for _, right in pairs})


def gram(blocks, pairs, shares, so_far=None, cost=0):
    rows, depth = blocks[0][0].shape
    chunks = len(blocks[0])
    flat = [chunk for block in blocks for chunk in block]
    more = so_far is not None
    tiles = len(pairs)
    left_rows, right_rows = sides(pairs)
    inputs = flat + ([so_far] if more else [])
    return pl.pallas_call(
        functools.partial(gram_kernel, pairs, chunks, more),
        in_specs=[pl.BlockSpec(memory_space=pltpu.VMEM)] * len(inputs),
        out_specs=pl.BlockSpec(memory_space=pltpu.VMEM),
        scratch_shapes=[
            pltpu.VMEM((len(side), rows, 3 * chunks * depth), jnp.bfloat16)
            for side in (left_rows, right_rows)
        ],
        out_shape=jax.ShapeDtypeStruct((shares, tiles, rows // shares, rows), jnp.float32),
        cost_estimate=pl.CostEstimate(flops=cost, bytes_accessed=0, transcendentals=0),
        name="gram",
    )(*inputs)


def in_vmem(kernel, inputs, outputs, name, tables=()):
    return pl.pallas_call(
        kernel,
        in_specs=[pl.BlockSpec(memory_space=pltpu.SMEM)] * len(tables)
        + [pl.BlockSpec(memory_space=pltpu.VMEM)] * len(inputs),
        out_specs=[pl.BlockSpec(memory_space=pltpu.VMEM)] * len(outputs),
        out_shape=[jax.ShapeDtypeStruct(shape, jnp.float32) for shape in outputs],
        cost_estimate=pl.CostEstimate(flops=0, bytes_accessed=1 << 20, transcendentals=0),
        name=name,
    )(*tables, *inputs)


def summed(moved, routes):
    def kernel(moved_ref, *outs):
        for out, (_, as_is, to_turn) in zip(outs, routes):
            for k, tile in enumerate(as_is + to_turn):
                out[k] = moved_ref[:, tile].sum(0)

    shape = moved.shape[2:]
    outputs = [(len(as_is + to_turn),) + shape for _, as_is, to_turn in routes]
    return in_vmem(kernel, [moved], outputs, "sum")


def turned(slabs, picks, shares):
    part, width = slabs[0].shape[1:]

    def kernel(*refs):
        *ins, out = refs
        rows = [ref[k] for ref, ks in zip(ins, picks) for k in ks]
        rows += [jnp.zeros((part, width), jnp.float32)] * (width // part - len(rows))
        out[...] = jnp.concatenate(rows, axis=0).T.reshape(out.shape)

    return in_vmem(kernel, slabs, [(shares, width // shares, width)], "turn")[0]


def assembled(table, slabs, picks, crossed, columns):
    shares, part, width = crossed.shape

    def kernel(table_ref, *refs):
        *ins, crossed_ref, out = refs
        pieces = [ref[k] for ref, ks in zip(ins, picks) for k in ks]
        for k in range(columns // width - len(pieces)):
            lanes = slice(k * part, (k + 1) * part)
            pieces.append(jnp.concatenate([crossed_ref[s, :, lanes] for s in range(shares)], axis=1))
        for slot, piece in enumerate(pieces):
            out[:, pl.ds(pl.multiple_of(table_ref[slot] * width, width), width)] = piece

    return in_vmem(kernel, [*slabs, crossed], [(part, columns)], "assemble", [table])[0]


def together(*values):
    return lax.optimization_barrier(values)


def on_device(three_index, coefficients):
    rows, aux, width = three_index.shape
    by_aux = three_index.transpose(1, 0, 2)
    blk, col = lax.axis_index("blk"), lax.axis_index("col")
    place, zh = col // ZH, col % ZH
    swap_zh = [(x * ZH + 1 - h, x * ZH + h) for x in range(X) for h in range(ZH)]
    shares = lax.axis_size("col")

    def over_x(part):
        moved = lax.all_to_all(
            part, "col", split_axis=0, concat_axis=0, tiled=True, axis_index_groups=X_GROUPS
        )
        return moved.reshape(X, part.shape[0] // X, rows, width)

    def to_other_half(value):
        return lax.ppermute(value, "col", swap_zh)

    def over_col(tiles):
        return lax.all_to_all(tiles, "col", split_axis=0, concat_axis=0, tiled=True)

    cut = aux - X
    ring = [coefficients.T]
    for step in range(1, X):
        route = [(((t + step) % X) * ZH + h, t * ZH + h) for t in range(X) for h in range(ZH)]
        ring.append(lax.ppermute(ring[0], "col", route))
    first, *ring = together(by_aux[:cut], *ring)
    ring = jnp.stack(ring)
    first_part = over_x(first)
    orbitals = lax.all_gather(ring, "blk", axis=0, tiled=False)
    last, first_part = together(by_aux[cut:], first_part)
    last_part = over_x(last)

    def to_send(part, k):
        return transformed(part, k, orbitals, place, 1 - zh)

    def kept(part, k):
        return transformed(part, k, orbitals, place, zh)

    def neighbours(own):
        return fetched(own, other_core), fetched(own, next_row), fetched(own, previous_row)

    arrived_0 = to_other_half(to_send(first_part, 0))
    arrived_1 = to_other_half(to_send(first_part, 1))
    own_0 = kept(first_part, 0) + arrived_0
    other_0, below_0, above_0 = neighbours(own_0)
    leaving_2, first_part = together(to_send(last_part, 0), first_part)
    arrived_2 = to_other_half(leaving_2)
    own_1 = kept(first_part, 1) + arrived_1
    own_2 = kept(last_part, 0) + arrived_2
    other_0, below_0, above_0, own_1 = together(other_0, below_0, above_0, own_1)
    across_0 = fetched(below_0, over_to_across)
    other_1, below_1, above_1 = neighbours(own_1)
    other_1, below_1, above_1, across_0, own_2 = together(other_1, below_1, above_1, across_0, own_2)
    across_1 = fetched(below_1, over_to_across)
    other_2, below_2, above_2 = neighbours(own_2)
    known = [(own_0, own_1), (other_0, other_1), (below_0, below_1), (above_0, above_1)]
    early = gram(known, EARLY, shares)
    other_2, below_2, above_2, across_1, early = together(other_2, below_2, above_2, across_1, early)
    across_2 = fetched(below_2, over_to_across)
    known_2 = [(own_2,), (other_2,), (below_2,), (above_2,)]
    early = gram(known_2, EARLY, shares, early)
    late = gram(known + [(across_0, across_1)], LATE, shares)
    early_moved = over_col(early)
    across_2, late, early = together(across_2, late, early)
    late = gram(known_2 + [(across_2,)], LATE, shares, late, LATE_COST)
    early_moved, late = together(early_moved, late)

    def sent_home(moved, routes):
        return [
            delivered(slab, RELATED[target]) if target else slab
            for slab, (target, _, _) in zip(summed(moved, routes), routes)
        ]

    late_moved, *slabs = together(over_col(late), *sent_home(early_moved, EARLY_ROUTES))
    slabs += sent_home(late_moved, LATE_ROUTES)
    straight = [range(len(as_is)) for _, as_is, _ in ROUTES]
    to_turn = [range(len(as_is), len(as_is + to_turn)) for _, as_is, to_turn in ROUTES]

    def chosen(picks):
        return [slab for slab, ks in zip(slabs, picks) if len(ks)], [ks for ks in picks if len(ks)]

    crossed = over_col(turned(*chosen(to_turn), shares))
    table = lax.dynamic_slice(jnp.asarray(column_table()), (blk, 0), (1, 16))[0]
    return assembled(table, *chosen(straight), crossed, rows * lax.axis_size("blk"))


def solution(mesh):
    return jax.shard_map(
        on_device,
        mesh=mesh,
        in_specs=(P("blk", None, "col"), P("col", "blk")),
        out_specs=P(("blk", "col"), None),
        check_vma=False,
    )
```

```python
import functools

import jax
import jax.numpy as jnp
import numpy as np
from jax import lax
from jax.experimental import pallas as pl
from jax.experimental.pallas import tpu as pltpu
from jax.sharding import PartitionSpec as P

Y, ZL, CORES, X, ZH = 4, 2, 2, 4, 2
X_GROUPS = [[x * ZH + zh for x in range(X)] for zh in range(ZH)]
OWN, OTHER, BELOW, ABOVE, ACROSS = range(5)
EARLY = [(OWN, OWN), (OWN, OTHER), (OWN, BELOW), (OTHER, BELOW), (BELOW, ABOVE)]
LATE = [(OWN, ACROSS), (OTHER, ACROSS), (BELOW, ACROSS), (ABOVE, ACROSS)]
EARLY_ROUTES = [(OWN, [0, 1, 2], []), (OTHER, [3], []), (BELOW, [4], [2, 3]), (ABOVE, [], [4])]
LATE_ROUTES = [(OWN, [0], []), (OTHER, [1], []), (BELOW, [2], []), (ABOVE, [3], []),
               (ACROSS, [], [0, 1, 2, 3])]
ROUTES = EARLY_ROUTES + LATE_ROUTES
LATE_COST = 20_000_000_000
SENT_COST = KEPT_COST = 5_000_000_000


def block_of(y, zl, core):
    return ((y % Y) * ZL + zl % ZL) * CORES + core % CORES


def upper(y):
    return (y % Y) // 2


def itself(y, zl, core):
    return y, zl, core


def other_core(y, zl, core):
    return y, zl, 1 - core


def next_row(y, zl, core):
    return y + 1, zl, core


def previous_row(y, zl, core):
    return y - 1, zl, (core + upper(y)) % 2


def next_across(y, zl, core):
    return y + 1, 1 - zl, (core + zl + upper(y)) % 2


def over_to_across(y, zl, core):
    return y, 1 - zl, (core + zl + upper(y)) % 2


RELATED = [itself, other_core, next_row, previous_row, next_across]


def places():
    return [(y, zl, core) for y in range(Y) for zl in range(ZL) for core in range(CORES)]


def fetched(value, source_of):
    route = [(block_of(*source_of(*at)), block_of(*at)) for at in places()]
    return lax.ppermute(value, "blk", route)


def delivered(value, target_of):
    route = [(block_of(*at), block_of(*target_of(*at))) for at in places()]
    return lax.ppermute(value, "blk", route)


def column_table():
    straight, turned = [], []
    for tiles, routes in ((EARLY, EARLY_ROUTES), (LATE, LATE_ROUTES)):
        for target, as_is, to_turn in routes:
            straight += [(target, tiles[k][1]) for k in as_is]
            turned += [(target, tiles[k][0]) for k in to_turn]
    table = np.zeros((len(places()), len(straight + turned)), np.int32)
    for slot, (target, column) in enumerate(straight + turned):
        for at in places():
            table[block_of(*RELATED[target](*at)), slot] = block_of(*RELATED[column](*at))
    return table


def high_and_low(value):
    high = value.astype(jnp.bfloat16)
    return high, (value - high.astype(jnp.float32)).astype(jnp.bfloat16)


def dot(left, right):
    return lax.dot_general(
        left, right, (((1,), (1,)), ((), ())), preferred_element_type=jnp.float32
    )


def transform_kernel(index, scalars, part, orbitals, out, rows_in, orbitals_in, sems):
    place, half = scalars[0], scalars[1]
    run, each, width = orbitals_in.shape[1:]
    copies = []
    for k in range(X):
        x = lax.rem(place + k, X)
        copies.append((
            pltpu.make_async_copy(part.at[x, index], rows_in.at[k], sems.at[0, k]),
            pltpu.make_async_copy(
                orbitals.at[pl.ds(half * run, run), k], orbitals_in.at[k], sems.at[1, k]
            ),
        ))
    for of_rows, of_orbitals in copies:
        of_rows.start()
        of_orbitals.start()
    for k, (of_rows, of_orbitals) in enumerate(copies):
        of_rows.wait()
        of_orbitals.wait()
        b_high, b_low = high_and_low(rows_in[k])
        c_high, c_low = high_and_low(orbitals_in[k].reshape(run * each, width))
        term = dot(b_high, c_high) + (dot(b_high, c_low) + dot(b_low, c_high))
        out[...] = out[...] + term if k else term


def transformed(part, index, orbitals, place, half, cost=0):
    rows, width = part.shape[2:]
    blocks, _, each, _ = orbitals.shape
    run = blocks // ZH
    return pl.pallas_call(
        functools.partial(transform_kernel, index),
        in_specs=[pl.BlockSpec(memory_space=pltpu.SMEM)] + [pl.BlockSpec(memory_space=pl.ANY)] * 2,
        out_specs=pl.BlockSpec(memory_space=pltpu.VMEM),
        out_shape=jax.ShapeDtypeStruct((rows, run * each), jnp.float32),
        scratch_shapes=[
            pltpu.VMEM((X, rows, width), jnp.float32),
            pltpu.VMEM((X, run, each, width), jnp.float32),
            pltpu.SemaphoreType.DMA((2, X)),
        ],
        cost_estimate=pl.CostEstimate(flops=cost, bytes_accessed=0, transcendentals=0),
        name="transform",
    )(jnp.stack([place, half]), part, orbitals)


def gram_kernel(pairs, chunks, more, *refs):
    left_rows, right_rows = sides(pairs)
    count = (1 + max(left_rows + right_rows)) * chunks
    blocks, refs = refs[:count], refs[count:]
    if more:
        so_far, refs = refs[0], refs[1:]
    out, lefts, rights = refs
    depth = blocks[0].shape[1]
    for k, block in enumerate(blocks):
        high, low = high_and_low(block[...])
        row, first = k // chunks, k % chunks * 3
        for ref, rows, order in (
            (lefts, left_rows, (high, high, low)), (rights, right_rows, (high, low, high))
        ):
            if row in rows:
                for piece, value in enumerate(order, first):
                    ref[rows.index(row), :, piece * depth : (piece + 1) * depth] = value

    shares, _, part, width = out.shape
    for t, (left, right) in enumerate(pairs):
        tile = dot(lefts[left_rows.index(left)], rights[right_rows.index(right)])
        tile = tile.reshape(shares, part, width)
        out[:, t] = so_far[:, t] + tile if more else tile


def sides(pairs):
    return sorted({left for left, _ in pairs}), sorted({right for _, right in pairs})


def gram(blocks, pairs, shares, so_far=None, cost=0):
    rows, depth = blocks[0][0].shape
    chunks = len(blocks[0])
    flat = [chunk for block in blocks for chunk in block]
    more = so_far is not None
    tiles = len(pairs)
    left_rows, right_rows = sides(pairs)
    inputs = flat + ([so_far] if more else [])
    return pl.pallas_call(
        functools.partial(gram_kernel, pairs, chunks, more),
        in_specs=[pl.BlockSpec(memory_space=pltpu.VMEM)] * len(inputs),
        out_specs=pl.BlockSpec(memory_space=pltpu.VMEM),
        scratch_shapes=[
            pltpu.VMEM((len(side), rows, 3 * chunks * depth), jnp.bfloat16)
            for side in (left_rows, right_rows)
        ],
        out_shape=jax.ShapeDtypeStruct((shares, tiles, rows // shares, rows), jnp.float32),
        cost_estimate=pl.CostEstimate(flops=cost, bytes_accessed=0, transcendentals=0),
        name="gram",
    )(*inputs)


def in_vmem(kernel, inputs, outputs, name, tables=()):
    return pl.pallas_call(
        kernel,
        in_specs=[pl.BlockSpec(memory_space=pltpu.SMEM)] * len(tables)
        + [pl.BlockSpec(memory_space=pltpu.VMEM)] * len(inputs),
        out_specs=[pl.BlockSpec(memory_space=pltpu.VMEM)] * len(outputs),
        out_shape=[jax.ShapeDtypeStruct(shape, jnp.float32) for shape in outputs],
        cost_estimate=pl.CostEstimate(flops=0, bytes_accessed=1 << 20, transcendentals=0),
        name=name,
    )(*tables, *inputs)


def summed(moved, routes):
    def kernel(moved_ref, *outs):
        for out, (_, as_is, to_turn) in zip(outs, routes):
            for k, tile in enumerate(as_is + to_turn):
                out[k] = moved_ref[:, tile].sum(0)

    shape = moved.shape[2:]
    outputs = [(len(as_is + to_turn),) + shape for _, as_is, to_turn in routes]
    return in_vmem(kernel, [moved], outputs, "sum")


def turned(slabs, picks, shares):
    part, width = slabs[0].shape[1:]

    def kernel(*refs):
        *ins, out = refs
        rows = [ref[k] for ref, ks in zip(ins, picks) for k in ks]
        rows += [jnp.zeros((part, width), jnp.float32)] * (width // part - len(rows))
        out[...] = jnp.concatenate(rows, axis=0).T.reshape(out.shape)

    return in_vmem(kernel, slabs, [(shares, width // shares, width)], "turn")[0]


def assembled(table, slabs, picks, crossed, columns):
    shares, part, width = crossed.shape

    def kernel(table_ref, *refs):
        *ins, crossed_ref, out = refs
        pieces = [ref[k] for ref, ks in zip(ins, picks) for k in ks]
        for k in range(columns // width - len(pieces)):
            lanes = slice(k * part, (k + 1) * part)
            pieces.append(jnp.concatenate([crossed_ref[s, :, lanes] for s in range(shares)], axis=1))
        for slot, piece in enumerate(pieces):
            out[:, pl.ds(pl.multiple_of(table_ref[slot] * width, width), width)] = piece

    return in_vmem(kernel, [*slabs, crossed], [(part, columns)], "assemble", [table])[0]


def together(*values):
    return lax.optimization_barrier(values)


def on_device(three_index, coefficients):
    rows, aux, width = three_index.shape
    by_aux = three_index.transpose(1, 0, 2)
    blk, col = lax.axis_index("blk"), lax.axis_index("col")
    place, zh = col // ZH, col % ZH
    swap_zh = [(x * ZH + 1 - h, x * ZH + h) for x in range(X) for h in range(ZH)]
    shares = lax.axis_size("col")

    def over_x(part):
        moved = lax.all_to_all(
            part, "col", split_axis=0, concat_axis=0, tiled=True, axis_index_groups=X_GROUPS
        )
        return moved.reshape(X, part.shape[0] // X, rows, width)

    def to_other_half(value):
        return lax.ppermute(value, "col", swap_zh)

    def over_col(tiles):
        return lax.all_to_all(tiles, "col", split_axis=0, concat_axis=0, tiled=True)

    cut = aux - X
    ring = [coefficients.T]
    for step in range(1, X):
        route = [(((t + step) % X) * ZH + h, t * ZH + h) for t in range(X) for h in range(ZH)]
        ring.append(lax.ppermute(ring[0], "col", route))
    first, *ring = together(by_aux[:cut], *ring)
    ring = jnp.stack(ring)
    first_part = over_x(first)
    orbitals = lax.all_gather(ring, "blk", axis=0, tiled=False)
    last, first_part = together(by_aux[cut:], first_part)
    last_part = over_x(last)

    def to_send(part, k):
        return transformed(part, k, orbitals, place, 1 - zh, SENT_COST)

    def kept(part, k):
        return transformed(part, k, orbitals, place, zh, KEPT_COST)

    def neighbours(own):
        return fetched(own, other_core), fetched(own, next_row), fetched(own, previous_row)

    arrived_0 = to_other_half(to_send(first_part, 0))
    arrived_1 = to_other_half(to_send(first_part, 1))
    own_0 = kept(first_part, 0) + arrived_0
    other_0, below_0, above_0 = neighbours(own_0)
    leaving_2, first_part = together(to_send(last_part, 0), first_part)
    arrived_2 = to_other_half(leaving_2)
    own_1 = kept(first_part, 1) + arrived_1
    own_2 = kept(last_part, 0) + arrived_2
    other_0, below_0, above_0, own_1 = together(other_0, below_0, above_0, own_1)
    across_0 = fetched(below_0, over_to_across)
    other_1, below_1, above_1 = neighbours(own_1)
    other_1, below_1, above_1, own_2 = together(other_1, below_1, above_1, own_2)
    across_1 = fetched(below_1, over_to_across)
    other_2, below_2, above_2 = neighbours(own_2)
    known = [(own_0, own_1), (other_0, other_1), (below_0, below_1), (above_0, above_1)]
    early = gram(known, EARLY, shares)
    other_2, below_2, above_2, across_0, early = together(other_2, below_2, above_2, across_0, early)
    across_2 = fetched(below_2, over_to_across)
    known_2 = [(own_2,), (other_2,), (below_2,), (above_2,)]
    early = gram(known_2, EARLY, shares, early)
    late = gram(known + [(across_0, across_1)], LATE, shares)
    early_moved = over_col(early)
    across_2, late, early = together(across_2, late, early)
    late = gram(known_2 + [(across_2,)], LATE, shares, late, LATE_COST)
    early_moved, late = together(early_moved, late)

    def sent_home(moved, routes):
        return [
            delivered(slab, RELATED[target]) if target else slab
            for slab, (target, _, _) in zip(summed(moved, routes), routes)
        ]

    late_moved, *slabs = together(over_col(late), *sent_home(early_moved, EARLY_ROUTES))
    slabs += sent_home(late_moved, LATE_ROUTES)
    straight = [range(len(as_is)) for _, as_is, _ in ROUTES]
    to_turn = [range(len(as_is), len(as_is + to_turn)) for _, as_is, to_turn in ROUTES]

    def chosen(picks):
        return [slab for slab, ks in zip(slabs, picks) if len(ks)], [ks for ks in picks if len(ks)]

    crossed = over_col(turned(*chosen(to_turn), shares))
    table = lax.dynamic_slice(jnp.asarray(column_table()), (blk, 0), (1, 16))[0]
    return assembled(table, *chosen(straight), crossed, rows * lax.axis_size("blk"))


def solution(mesh):
    return jax.shard_map(
        on_device,
        mesh=mesh,
        in_specs=(P("blk", None, "col"), P("col", "blk")),
        out_specs=P(("blk", "col"), None),
        check_vma=False,
    )
```

```python
import functools

import jax
import jax.numpy as jnp
import numpy as np
from jax import lax
from jax.experimental import pallas as pl
from jax.experimental.pallas import tpu as pltpu
from jax.sharding import PartitionSpec as P

Y, ZL, CORES, X, ZH = 4, 2, 2, 4, 2
X_GROUPS = [[x * ZH + zh for x in range(X)] for zh in range(ZH)]
OWN, OTHER, BELOW, ABOVE, ACROSS = range(5)
EARLY = [(OWN, OWN), (OWN, OTHER), (OWN, BELOW), (OTHER, BELOW), (BELOW, ABOVE)]
LATE = [(OWN, ACROSS), (OTHER, ACROSS), (BELOW, ACROSS), (ABOVE, ACROSS)]
EARLY_ROUTES = [(OWN, [0, 1, 2], []), (OTHER, [3], []), (BELOW, [4], [2, 3]), (ABOVE, [], [4])]
LATE_ROUTES = [(OWN, [0], []), (OTHER, [1], []), (BELOW, [2], []), (ABOVE, [3], []),
               (ACROSS, [], [0, 1, 2, 3])]
ROUTES = EARLY_ROUTES + LATE_ROUTES
LATE_COST = 20_000_000_000
SENT_COST = KEPT_COST = 5_000_000_000


def block_of(y, zl, core):
    return ((y % Y) * ZL + zl % ZL) * CORES + core % CORES


def upper(y):
    return (y % Y) // 2


def itself(y, zl, core):
    return y, zl, core


def other_core(y, zl, core):
    return y, zl, 1 - core


def next_row(y, zl, core):
    return y + 1, zl, core


def previous_row(y, zl, core):
    return y - 1, zl, (core + upper(y)) % 2


def next_across(y, zl, core):
    return y + 1, 1 - zl, (core + zl + upper(y)) % 2


def over_to_across(y, zl, core):
    return y, 1 - zl, (core + zl + upper(y)) % 2


RELATED = [itself, other_core, next_row, previous_row, next_across]


def places():
    return [(y, zl, core) for y in range(Y) for zl in range(ZL) for core in range(CORES)]


def fetched(value, source_of):
    route = [(block_of(*source_of(*at)), block_of(*at)) for at in places()]
    return lax.ppermute(value, "blk", route)


def delivered(value, target_of):
    route = [(block_of(*at), block_of(*target_of(*at))) for at in places()]
    return lax.ppermute(value, "blk", route)


def column_table():
    straight, turned = [], []
    for tiles, routes in ((EARLY, EARLY_ROUTES), (LATE, LATE_ROUTES)):
        for target, as_is, to_turn in routes:
            straight += [(target, tiles[k][1]) for k in as_is]
            turned += [(target, tiles[k][0]) for k in to_turn]
    table = np.zeros((len(places()), len(straight + turned)), np.int32)
    for slot, (target, column) in enumerate(straight + turned):
        for at in places():
            table[block_of(*RELATED[target](*at)), slot] = block_of(*RELATED[column](*at))
    return table


def high_and_low(value):
    high = value.astype(jnp.bfloat16)
    return high, (value - high.astype(jnp.float32)).astype(jnp.bfloat16)


def dot(left, right):
    return lax.dot_general(
        left, right, (((1,), (1,)), ((), ())), preferred_element_type=jnp.float32
    )


def transform_kernel(index, keeps, part, orbitals, out, rows_in, orbitals_in, sems):
    col = lax.axis_index("col")
    place, half = col // ZH, lax.rem(col + (0 if keeps else 1), ZH)
    run, each, width = orbitals_in.shape[1:]
    copies = []
    for k in range(X):
        x = lax.rem(place + k, X)
        copies.append((
            pltpu.make_async_copy(part.at[x, index], rows_in.at[k], sems.at[0, k]),
            pltpu.make_async_copy(
                orbitals.at[pl.ds(half * run, run), k], orbitals_in.at[k], sems.at[1, k]
            ),
        ))
    for of_rows, of_orbitals in copies:
        of_rows.start()
        of_orbitals.start()
    for k, (of_rows, of_orbitals) in enumerate(copies):
        of_rows.wait()
        of_orbitals.wait()
        b_high, b_low = high_and_low(rows_in[k])
        c_high, c_low = high_and_low(orbitals_in[k].reshape(run * each, width))
        term = dot(b_high, c_high) + (dot(b_high, c_low) + dot(b_low, c_high))
        out[...] = out[...] + term if k else term


def transformed(part, index, orbitals, keeps, cost):
    rows, width = part.shape[2:]
    blocks, _, each, _ = orbitals.shape
    run = blocks // ZH
    return pl.pallas_call(
        functools.partial(transform_kernel, index, keeps),
        in_specs=[pl.BlockSpec(memory_space=pl.ANY)] * 2,
        out_specs=pl.BlockSpec(memory_space=pltpu.VMEM),
        out_shape=jax.ShapeDtypeStruct((rows, run * each), jnp.float32),
        scratch_shapes=[
            pltpu.VMEM((X, rows, width), jnp.float32),
            pltpu.VMEM((X, run, each, width), jnp.float32),
            pltpu.SemaphoreType.DMA((2, X)),
        ],
        cost_estimate=pl.CostEstimate(flops=cost, bytes_accessed=0, transcendentals=0),
        name="transform",
    )(part, orbitals)


def gram_kernel(pairs, chunks, more, *refs):
    left_rows, right_rows = sides(pairs)
    count = (1 + max(left_rows + right_rows)) * chunks
    blocks, refs = refs[:count], refs[count:]
    if more:
        so_far, refs = refs[0], refs[1:]
    out, lefts, rights = refs
    depth = blocks[0].shape[1]
    for k, block in enumerate(blocks):
        high, low = high_and_low(block[...])
        row, first = k // chunks, k % chunks * 3
        for ref, rows, order in (
            (lefts, left_rows, (high, high, low)), (rights, right_rows, (high, low, high))
        ):
            if row in rows:
                for piece, value in enumerate(order, first):
                    ref[rows.index(row), :, piece * depth : (piece + 1) * depth] = value

    shares, _, part, width = out.shape
    for t, (left, right) in enumerate(pairs):
        tile = dot(lefts[left_rows.index(left)], rights[right_rows.index(right)])
        tile = tile.reshape(shares, part, width)
        out[:, t] = so_far[:, t] + tile if more else tile


def sides(pairs):
    return sorted({left for left, _ in pairs}), sorted({right for _, right in pairs})


def gram(blocks, pairs, shares, so_far=None, cost=0):
    rows, depth = blocks[0][0].shape
    chunks = len(blocks[0])
    flat = [chunk for block in blocks for chunk in block]
    more = so_far is not None
    tiles = len(pairs)
    left_rows, right_rows = sides(pairs)
    inputs = flat + ([so_far] if more else [])
    return pl.pallas_call(
        functools.partial(gram_kernel, pairs, chunks, more),
        in_specs=[pl.BlockSpec(memory_space=pltpu.VMEM)] * len(inputs),
        out_specs=pl.BlockSpec(memory_space=pltpu.VMEM),
        scratch_shapes=[
            pltpu.VMEM((len(side), rows, 3 * chunks * depth), jnp.bfloat16)
            for side in (left_rows, right_rows)
        ],
        out_shape=jax.ShapeDtypeStruct((shares, tiles, rows // shares, rows), jnp.float32),
        cost_estimate=pl.CostEstimate(flops=cost, bytes_accessed=0, transcendentals=0),
        name="gram",
    )(*inputs)


def in_vmem(kernel, inputs, outputs, name, tables=()):
    return pl.pallas_call(
        kernel,
        in_specs=[pl.BlockSpec(memory_space=pltpu.SMEM)] * len(tables)
        + [pl.BlockSpec(memory_space=pltpu.VMEM)] * len(inputs),
        out_specs=[pl.BlockSpec(memory_space=pltpu.VMEM)] * len(outputs),
        out_shape=[jax.ShapeDtypeStruct(shape, jnp.float32) for shape in outputs],
        cost_estimate=pl.CostEstimate(flops=0, bytes_accessed=1 << 20, transcendentals=0),
        name=name,
    )(*tables, *inputs)


def summed(moved, routes):
    def kernel(moved_ref, *outs):
        for out, (_, as_is, to_turn) in zip(outs, routes):
            for k, tile in enumerate(as_is + to_turn):
                out[k] = moved_ref[:, tile].sum(0)

    shape = moved.shape[2:]
    outputs = [(len(as_is + to_turn),) + shape for _, as_is, to_turn in routes]
    return in_vmem(kernel, [moved], outputs, "sum")


def turned(slabs, picks, shares):
    part, width = slabs[0].shape[1:]

    def kernel(*refs):
        *ins, out = refs
        rows = [ref[k] for ref, ks in zip(ins, picks) for k in ks]
        rows += [jnp.zeros((part, width), jnp.float32)] * (width // part - len(rows))
        out[...] = jnp.concatenate(rows, axis=0).T.reshape(out.shape)

    return in_vmem(kernel, slabs, [(shares, width // shares, width)], "turn")[0]


def assembled(table, slabs, picks, crossed, columns):
    shares, part, width = crossed.shape

    def kernel(table_ref, *refs):
        *ins, crossed_ref, out = refs
        pieces = [ref[k] for ref, ks in zip(ins, picks) for k in ks]
        for k in range(columns // width - len(pieces)):
            lanes = slice(k * part, (k + 1) * part)
            pieces.append(jnp.concatenate([crossed_ref[s, :, lanes] for s in range(shares)], axis=1))
        for slot, piece in enumerate(pieces):
            out[:, pl.ds(pl.multiple_of(table_ref[slot] * width, width), width)] = piece

    return in_vmem(kernel, [*slabs, crossed], [(part, columns)], "assemble", [table])[0]


def together(*values):
    return lax.optimization_barrier(values)


def on_device(three_index, coefficients):
    rows, aux, width = three_index.shape
    by_aux = three_index.transpose(1, 0, 2)
    blk = lax.axis_index("blk")
    swap_zh = [(x * ZH + 1 - h, x * ZH + h) for x in range(X) for h in range(ZH)]
    shares = lax.axis_size("col")

    def over_x(part):
        moved = lax.all_to_all(
            part, "col", split_axis=0, concat_axis=0, tiled=True, axis_index_groups=X_GROUPS
        )
        return moved.reshape(X, part.shape[0] // X, rows, width)

    def to_other_half(value):
        return lax.ppermute(value, "col", swap_zh)

    def over_col(tiles):
        return lax.all_to_all(tiles, "col", split_axis=0, concat_axis=0, tiled=True)

    cut = aux - X
    ring = [coefficients.T]
    for step in range(1, X):
        route = [(((t + step) % X) * ZH + h, t * ZH + h) for t in range(X) for h in range(ZH)]
        ring.append(lax.ppermute(ring[0], "col", route))
    first, *ring = together(by_aux[:cut], *ring)
    ring = jnp.stack(ring)
    first_part = over_x(first)
    orbitals = lax.all_gather(ring, "blk", axis=0, tiled=False)
    last, first_part = together(by_aux[cut:], first_part)
    last_part = over_x(last)

    def to_send(part, k):
        return transformed(part, k, orbitals, False, SENT_COST)

    def kept(part, k):
        return transformed(part, k, orbitals, True, KEPT_COST)

    def neighbours(own):
        return fetched(own, other_core), fetched(own, next_row), fetched(own, previous_row)

    arrived_0 = to_other_half(to_send(first_part, 0))
    arrived_1 = to_other_half(to_send(first_part, 1))
    own_0 = kept(first_part, 0) + arrived_0
    other_0, below_0, above_0 = neighbours(own_0)
    leaving_2, first_part = together(to_send(last_part, 0), first_part)
    arrived_2 = to_other_half(leaving_2)
    own_1 = kept(first_part, 1) + arrived_1
    own_2 = kept(last_part, 0) + arrived_2
    other_0, below_0, above_0, own_1 = together(other_0, below_0, above_0, own_1)
    across_0 = fetched(below_0, over_to_across)
    other_1, below_1, above_1 = neighbours(own_1)
    other_1, below_1, above_1, own_2 = together(other_1, below_1, above_1, own_2)
    across_0, below_1 = together(across_0, below_1)
    across_1 = fetched(below_1, over_to_across)
    other_2, below_2, above_2 = neighbours(own_2)
    known = [(own_0, own_1), (other_0, other_1), (below_0, below_1), (above_0, above_1)]
    early = gram(known, EARLY, shares)
    other_2, below_2, above_2, across_0, early = together(other_2, below_2, above_2, across_0, early)
    across_2 = fetched(below_2, over_to_across)
    known_2 = [(own_2,), (other_2,), (below_2,), (above_2,)]
    early = gram(known_2, EARLY, shares, early)
    late = gram(known + [(across_0, across_1)], LATE, shares)
    early_moved = over_col(early)
    across_2, late, early = together(across_2, late, early)
    late = gram(known_2 + [(across_2,)], LATE, shares, late, LATE_COST)
    early_moved, late = together(early_moved, late)

    def sent_home(moved, routes):
        return [
            delivered(slab, RELATED[target]) if target else slab
            for slab, (target, _, _) in zip(summed(moved, routes), routes)
        ]

    late_moved, *slabs = together(over_col(late), *sent_home(early_moved, EARLY_ROUTES))
    slabs += sent_home(late_moved, LATE_ROUTES)
    straight = [range(len(as_is)) for _, as_is, _ in ROUTES]
    to_turn = [range(len(as_is), len(as_is + to_turn)) for _, as_is, to_turn in ROUTES]

    def chosen(picks):
        return [slab for slab, ks in zip(slabs, picks) if len(ks)], [ks for ks in picks if len(ks)]

    crossed = over_col(turned(*chosen(to_turn), shares))
    table = lax.dynamic_slice(jnp.asarray(column_table()), (blk, 0), (1, 16))[0]
    return assembled(table, *chosen(straight), crossed, rows * lax.axis_size("blk"))


def solution(mesh):
    return jax.shard_map(
        on_device,
        mesh=mesh,
        in_specs=(P("blk", None, "col"), P("col", "blk")),
        out_specs=P(("blk", "col"), None),
        check_vma=False,
    )
```

```python
import functools

import jax
import jax.numpy as jnp
import numpy as np
from jax import lax
from jax.experimental import pallas as pl
from jax.experimental.pallas import tpu as pltpu
from jax.sharding import PartitionSpec as P

Y, ZL, CORES, X, ZH = 4, 2, 2, 4, 2
X_GROUPS = [[x * ZH + zh for x in range(X)] for zh in range(ZH)]
OWN, OTHER, BELOW, ABOVE, ACROSS = range(5)
EARLY = [(OWN, OWN), (OWN, OTHER), (OWN, BELOW), (OTHER, BELOW), (BELOW, ABOVE)]
LATE = [(OWN, ACROSS), (OTHER, ACROSS), (BELOW, ACROSS), (ABOVE, ACROSS)]
EARLY_ROUTES = [(OWN, [0, 1, 2], []), (OTHER, [3], []), (BELOW, [4], [2, 3]), (ABOVE, [], [4])]
LATE_ROUTES = [(OWN, [0], []), (OTHER, [1], []), (BELOW, [2], []), (ABOVE, [3], []),
               (ACROSS, [], [0, 1, 2, 3])]
ROUTES = EARLY_ROUTES + LATE_ROUTES
LATE_COST = 20_000_000_000
SENT_COST = KEPT_COST = 5_000_000_000


def block_of(y, zl, core):
    return ((y % Y) * ZL + zl % ZL) * CORES + core % CORES


def upper(y):
    return (y % Y) // 2


def itself(y, zl, core):
    return y, zl, core


def other_core(y, zl, core):
    return y, zl, 1 - core


def next_row(y, zl, core):
    return y + 1, zl, core


def previous_row(y, zl, core):
    return y - 1, zl, (core + upper(y)) % 2


def next_across(y, zl, core):
    return y + 1, 1 - zl, (core + zl + upper(y)) % 2


def over_to_across(y, zl, core):
    return y, 1 - zl, (core + zl + upper(y)) % 2


RELATED = [itself, other_core, next_row, previous_row, next_across]


def places():
    return [(y, zl, core) for y in range(Y) for zl in range(ZL) for core in range(CORES)]


def fetched(value, source_of):
    route = [(block_of(*source_of(*at)), block_of(*at)) for at in places()]
    return lax.ppermute(value, "blk", route)


def delivered(value, target_of):
    route = [(block_of(*at), block_of(*target_of(*at))) for at in places()]
    return lax.ppermute(value, "blk", route)


def column_table():
    straight, turned = [], []
    for tiles, routes in ((EARLY, EARLY_ROUTES), (LATE, LATE_ROUTES)):
        for target, as_is, to_turn in routes:
            straight += [(target, tiles[k][1]) for k in as_is]
            turned += [(target, tiles[k][0]) for k in to_turn]
    table = np.zeros((len(places()), len(straight + turned)), np.int32)
    for slot, (target, column) in enumerate(straight + turned):
        for at in places():
            table[block_of(*RELATED[target](*at)), slot] = block_of(*RELATED[column](*at))
    return table


def high_and_low(value):
    high = value.astype(jnp.bfloat16)
    return high, (value - high.astype(jnp.float32)).astype(jnp.bfloat16)


def dot(left, right):
    return lax.dot_general(
        left, right, (((1,), (1,)), ((), ())), preferred_element_type=jnp.float32
    )


def transform_kernel(index, keeps, part, orbitals, out, rows_in, orbitals_in, sems):
    col = lax.axis_index("col")
    place, half = col // ZH, lax.rem(col + (0 if keeps else 1), ZH)
    run, each, width = orbitals_in.shape[1:]
    copies = []
    for k in range(X):
        x = lax.rem(place + k, X)
        copies.append((
            pltpu.make_async_copy(part.at[x, index], rows_in.at[k], sems.at[0, k]),
            pltpu.make_async_copy(
                orbitals.at[pl.ds(half * run, run), k], orbitals_in.at[k], sems.at[1, k]
            ),
        ))
    for of_rows, of_orbitals in copies:
        of_rows.start()
        of_orbitals.start()
    for k, (of_rows, of_orbitals) in enumerate(copies):
        of_rows.wait()
        of_orbitals.wait()
        b_high, b_low = high_and_low(rows_in[k])
        c_high, c_low = high_and_low(orbitals_in[k].reshape(run * each, width))
        term = dot(b_high, c_high) + (dot(b_high, c_low) + dot(b_low, c_high))
        out[...] = out[...] + term if k else term


def transformed(part, index, orbitals, keeps, cost):
    rows, width = part.shape[2:]
    blocks, _, each, _ = orbitals.shape
    run = blocks // ZH
    return pl.pallas_call(
        functools.partial(transform_kernel, index, keeps),
        in_specs=[pl.BlockSpec(memory_space=pl.ANY)] * 2,
        out_specs=pl.BlockSpec(memory_space=pltpu.VMEM),
        out_shape=jax.ShapeDtypeStruct((rows, run * each), jnp.float32),
        scratch_shapes=[
            pltpu.VMEM((X, rows, width), jnp.float32),
            pltpu.VMEM((X, run, each, width), jnp.float32),
            pltpu.SemaphoreType.DMA((2, X)),
        ],
        cost_estimate=pl.CostEstimate(flops=cost, bytes_accessed=0, transcendentals=0),
        name="transform",
    )(part, orbitals)


def gram_kernel(pairs, chunks, more, *refs):
    left_rows, right_rows = sides(pairs)
    count = (1 + max(left_rows + right_rows)) * chunks
    blocks, refs = refs[:count], refs[count:]
    if more:
        so_far, refs = refs[0], refs[1:]
    out, lefts, rights = refs
    depth = blocks[0].shape[1]
    for k, block in enumerate(blocks):
        high, low = high_and_low(block[...])
        row, first = k // chunks, k % chunks * 3
        for ref, rows, order in (
            (lefts, left_rows, (high, high, low)), (rights, right_rows, (high, low, high))
        ):
            if row in rows:
                for piece, value in enumerate(order, first):
                    ref[rows.index(row), :, piece * depth : (piece + 1) * depth] = value

    shares, _, part, width = out.shape
    for t, (left, right) in enumerate(pairs):
        tile = dot(lefts[left_rows.index(left)], rights[right_rows.index(right)])
        tile = tile.reshape(shares, part, width)
        out[:, t] = so_far[:, t] + tile if more else tile


def sides(pairs):
    return sorted({left for left, _ in pairs}), sorted({right for _, right in pairs})


def gram(blocks, pairs, shares, so_far=None, cost=0):
    rows, depth = blocks[0][0].shape
    chunks = len(blocks[0])
    flat = [chunk for block in blocks for chunk in block]
    more = so_far is not None
    tiles = len(pairs)
    left_rows, right_rows = sides(pairs)
    inputs = flat + ([so_far] if more else [])
    return pl.pallas_call(
        functools.partial(gram_kernel, pairs, chunks, more),
        in_specs=[pl.BlockSpec(memory_space=pltpu.VMEM)] * len(inputs),
        out_specs=pl.BlockSpec(memory_space=pltpu.VMEM),
        scratch_shapes=[
            pltpu.VMEM((len(side), rows, 3 * chunks * depth), jnp.bfloat16)
            for side in (left_rows, right_rows)
        ],
        out_shape=jax.ShapeDtypeStruct((shares, tiles, rows // shares, rows), jnp.float32),
        cost_estimate=pl.CostEstimate(flops=cost, bytes_accessed=0, transcendentals=0),
        name="gram",
    )(*inputs)


def in_vmem(kernel, inputs, outputs, name, tables=()):
    return pl.pallas_call(
        kernel,
        in_specs=[pl.BlockSpec(memory_space=pltpu.SMEM)] * len(tables)
        + [pl.BlockSpec(memory_space=pltpu.VMEM)] * len(inputs),
        out_specs=[pl.BlockSpec(memory_space=pltpu.VMEM)] * len(outputs),
        out_shape=[jax.ShapeDtypeStruct(shape, jnp.float32) for shape in outputs],
        cost_estimate=pl.CostEstimate(flops=0, bytes_accessed=1 << 20, transcendentals=0),
        name=name,
    )(*tables, *inputs)


def summed(moved, routes):
    def kernel(moved_ref, *outs):
        for out, (_, as_is, to_turn) in zip(outs, routes):
            for k, tile in enumerate(as_is + to_turn):
                out[k] = moved_ref[:, tile].sum(0)

    shape = moved.shape[2:]
    outputs = [(len(as_is + to_turn),) + shape for _, as_is, to_turn in routes]
    return in_vmem(kernel, [moved], outputs, "sum")


def turned(slabs, picks, shares):
    part, width = slabs[0].shape[1:]

    def kernel(*refs):
        *ins, out = refs
        rows = [ref[k] for ref, ks in zip(ins, picks) for k in ks]
        rows += [jnp.zeros((part, width), jnp.float32)] * (width // part - len(rows))
        out[...] = jnp.concatenate(rows, axis=0).T.reshape(out.shape)

    return in_vmem(kernel, slabs, [(shares, width // shares, width)], "turn")[0]


def assembled(table, slabs, picks, crossed, columns):
    shares, part, width = crossed.shape

    def kernel(table_ref, *refs):
        *ins, crossed_ref, out = refs
        pieces = [ref[k] for ref, ks in zip(ins, picks) for k in ks]
        for k in range(columns // width - len(pieces)):
            lanes = slice(k * part, (k + 1) * part)
            pieces.append(jnp.concatenate([crossed_ref[s, :, lanes] for s in range(shares)], axis=1))
        for slot, piece in enumerate(pieces):
            out[:, pl.ds(pl.multiple_of(table_ref[slot] * width, width), width)] = piece

    return in_vmem(kernel, [*slabs, crossed], [(part, columns)], "assemble", [table])[0]


def together(*values):
    return lax.optimization_barrier(values)


def on_device(three_index, coefficients):
    rows, aux, width = three_index.shape
    by_aux = three_index.transpose(1, 0, 2)
    blk = lax.axis_index("blk")
    swap_zh = [(x * ZH + 1 - h, x * ZH + h) for x in range(X) for h in range(ZH)]
    shares = lax.axis_size("col")

    def over_x(part):
        moved = lax.all_to_all(
            part, "col", split_axis=0, concat_axis=0, tiled=True, axis_index_groups=X_GROUPS
        )
        return moved.reshape(X, part.shape[0] // X, rows, width)

    def to_other_half(value):
        return lax.ppermute(value, "col", swap_zh)

    def over_col(tiles):
        return lax.all_to_all(tiles, "col", split_axis=0, concat_axis=0, tiled=True)

    cut = aux - X
    ring = [coefficients.T]
    for step in range(1, X):
        route = [(((t + step) % X) * ZH + h, t * ZH + h) for t in range(X) for h in range(ZH)]
        ring.append(lax.ppermute(ring[0], "col", route))
    first, *ring = together(by_aux[:cut], *ring)
    ring = jnp.stack(ring)
    first_part = over_x(first)
    orbitals = lax.all_gather(ring, "blk", axis=0, tiled=False)
    last, first_part = together(by_aux[cut:], first_part)
    last_part = over_x(last)

    def to_send(part, k):
        return transformed(part, k, orbitals, False, SENT_COST)

    def kept(part, k):
        return transformed(part, k, orbitals, True, KEPT_COST)

    def neighbours(own):
        return fetched(own, other_core), fetched(own, next_row), fetched(own, previous_row)

    arrived_0 = to_other_half(to_send(first_part, 0))
    arrived_1 = to_other_half(to_send(first_part, 1))
    kept_1, arrived_0 = together(kept(first_part, 1), arrived_0)
    own_0 = kept(first_part, 0) + arrived_0
    other_0, below_0, above_0 = neighbours(own_0)
    arrived_2 = to_other_half(to_send(last_part, 0))
    own_1 = kept_1 + arrived_1
    own_2 = kept(last_part, 0) + arrived_2
    other_0, below_0, above_0, own_1 = together(other_0, below_0, above_0, own_1)
    across_0 = fetched(below_0, over_to_across)
    other_1, below_1, above_1 = neighbours(own_1)
    other_1, below_1, above_1, own_2 = together(other_1, below_1, above_1, own_2)
    across_0, below_1 = together(across_0, below_1)
    across_1 = fetched(below_1, over_to_across)
    other_2, below_2, above_2 = neighbours(own_2)
    known = [(own_0, own_1), (other_0, other_1), (below_0, below_1), (above_0, above_1)]
    early = gram(known, EARLY, shares)
    other_2, below_2, above_2, across_0, early = together(other_2, below_2, above_2, across_0, early)
    across_2 = fetched(below_2, over_to_across)
    known_2 = [(own_2,), (other_2,), (below_2,), (above_2,)]
    early = gram(known_2, EARLY, shares, early)
    late = gram(known + [(across_0, across_1)], LATE, shares)
    early_moved = over_col(early)
    across_2, late, early = together(across_2, late, early)
    late = gram(known_2 + [(across_2,)], LATE, shares, late, LATE_COST)
    early_moved, late = together(early_moved, late)

    def sent_home(moved, routes):
        return [
            delivered(slab, RELATED[target]) if target else slab
            for slab, (target, _, _) in zip(summed(moved, routes), routes)
        ]

    late_moved, *slabs = together(over_col(late), *sent_home(early_moved, EARLY_ROUTES))
    slabs += sent_home(late_moved, LATE_ROUTES)
    straight = [range(len(as_is)) for _, as_is, _ in ROUTES]
    to_turn = [range(len(as_is), len(as_is + to_turn)) for _, as_is, to_turn in ROUTES]

    def chosen(picks):
        return [slab for slab, ks in zip(slabs, picks) if len(ks)], [ks for ks in picks if len(ks)]

    crossed = over_col(turned(*chosen(to_turn), shares))
    table = lax.dynamic_slice(jnp.asarray(column_table()), (blk, 0), (1, 16))[0]
    return assembled(table, *chosen(straight), crossed, rows * lax.axis_size("blk"))


def solution(mesh):
    return jax.shard_map(
        on_device,
        mesh=mesh,
        in_specs=(P("blk", None, "col"), P("col", "blk")),
        out_specs=P(("blk", "col"), None),
        check_vma=False,
    )
```

```python
import functools

import jax
import jax.numpy as jnp
import numpy as np
from jax import lax
from jax.experimental import pallas as pl
from jax.experimental.pallas import tpu as pltpu
from jax.sharding import PartitionSpec as P

Y, ZL, CORES, X, ZH = 4, 2, 2, 4, 2
X_GROUPS = [[x * ZH + zh for x in range(X)] for zh in range(ZH)]
OWN, OTHER, BELOW, ABOVE, ACROSS = range(5)
EARLY = [(OWN, OWN), (OWN, OTHER), (OWN, BELOW), (OTHER, BELOW), (BELOW, ABOVE)]
LATE = [(OWN, ACROSS), (OTHER, ACROSS), (BELOW, ACROSS), (ABOVE, ACROSS)]
EARLY_ROUTES = [(OWN, [0, 1, 2], []), (OTHER, [3], []), (BELOW, [4], [2, 3]), (ABOVE, [], [4])]
LATE_ROUTES = [(OWN, [0], []), (OTHER, [1], []), (BELOW, [2], []), (ABOVE, [3], []),
               (ACROSS, [], [0, 1, 2, 3])]
ROUTES = EARLY_ROUTES + LATE_ROUTES
LATE_COST = 20_000_000_000
SENT_COST = KEPT_COST = 5_000_000_000


def block_of(y, zl, core):
    return ((y % Y) * ZL + zl % ZL) * CORES + core % CORES


def upper(y):
    return (y % Y) // 2


def itself(y, zl, core):
    return y, zl, core


def other_core(y, zl, core):
    return y, zl, 1 - core


def next_row(y, zl, core):
    return y + 1, zl, core


def previous_row(y, zl, core):
    return y - 1, zl, (core + upper(y)) % 2


def next_across(y, zl, core):
    return y + 1, 1 - zl, (core + zl + upper(y)) % 2


def over_to_across(y, zl, core):
    return y, 1 - zl, (core + zl + upper(y)) % 2


RELATED = [itself, other_core, next_row, previous_row, next_across]


def places():
    return [(y, zl, core) for y in range(Y) for zl in range(ZL) for core in range(CORES)]


def fetched(value, source_of):
    route = [(block_of(*source_of(*at)), block_of(*at)) for at in places()]
    return lax.ppermute(value, "blk", route)


def delivered(value, target_of):
    route = [(block_of(*at), block_of(*target_of(*at))) for at in places()]
    return lax.ppermute(value, "blk", route)


def column_table():
    straight, turned = [], []
    for tiles, routes in ((EARLY, EARLY_ROUTES), (LATE, LATE_ROUTES)):
        for target, as_is, to_turn in routes:
            straight += [(target, tiles[k][1]) for k in as_is]
            turned += [(target, tiles[k][0]) for k in to_turn]
    table = np.zeros((len(places()), len(straight + turned)), np.int32)
    for slot, (target, column) in enumerate(straight + turned):
        for at in places():
            table[block_of(*RELATED[target](*at)), slot] = block_of(*RELATED[column](*at))
    return table


def high_and_low(value):
    high = value.astype(jnp.bfloat16)
    return high, (value - high.astype(jnp.float32)).astype(jnp.bfloat16)


def dot(left, right):
    return lax.dot_general(
        left, right, (((1,), (1,)), ((), ())), preferred_element_type=jnp.float32
    )


def transform_kernel(index, keeps, part, orbitals, out, rows_in, orbitals_in, sems):
    col = lax.axis_index("col")
    place, half = col // ZH, lax.rem(col + (0 if keeps else 1), ZH)
    run, each, width = orbitals_in.shape[1:]
    copies = []
    for k in range(X):
        x = lax.rem(place + k, X)
        copies.append((
            pltpu.make_async_copy(part.at[x, index], rows_in.at[k], sems.at[0, k]),
            pltpu.make_async_copy(
                orbitals.at[pl.ds(half * run, run), k], orbitals_in.at[k], sems.at[1, k]
            ),
        ))
    for of_rows, of_orbitals in copies:
        of_rows.start()
        of_orbitals.start()
    for k, (of_rows, of_orbitals) in enumerate(copies):
        of_rows.wait()
        of_orbitals.wait()
        b_high, b_low = high_and_low(rows_in[k])
        c_high, c_low = high_and_low(orbitals_in[k].reshape(run * each, width))
        term = dot(b_high, c_high) + (dot(b_high, c_low) + dot(b_low, c_high))
        out[...] = out[...] + term if k else term


def transformed(part, index, orbitals, keeps, cost):
    rows, width = part.shape[2:]
    blocks, _, each, _ = orbitals.shape
    run = blocks // ZH
    return pl.pallas_call(
        functools.partial(transform_kernel, index, keeps),
        in_specs=[pl.BlockSpec(memory_space=pl.ANY)] * 2,
        out_specs=pl.BlockSpec(memory_space=pltpu.VMEM),
        out_shape=jax.ShapeDtypeStruct((rows, run * each), jnp.float32),
        scratch_shapes=[
            pltpu.VMEM((X, rows, width), jnp.float32),
            pltpu.VMEM((X, run, each, width), jnp.float32),
            pltpu.SemaphoreType.DMA((2, X)),
        ],
        cost_estimate=pl.CostEstimate(flops=cost, bytes_accessed=0, transcendentals=0),
        name="transform",
    )(part, orbitals)


def gram_kernel(pairs, chunks, more, *refs):
    left_rows, right_rows = sides(pairs)
    count = (1 + max(left_rows + right_rows)) * chunks
    blocks, refs = refs[:count], refs[count:]
    if more:
        so_far, refs = refs[0], refs[1:]
    out, lefts, rights = refs
    depth = blocks[0].shape[1]
    for k, block in enumerate(blocks):
        high, low = high_and_low(block[...])
        row, first = k // chunks, k % chunks * 3
        for ref, rows, order in (
            (lefts, left_rows, (high, high, low)), (rights, right_rows, (high, low, high))
        ):
            if row in rows:
                for piece, value in enumerate(order, first):
                    ref[rows.index(row), :, piece * depth : (piece + 1) * depth] = value

    shares, _, part, width = out.shape
    for t, (left, right) in enumerate(pairs):
        tile = dot(lefts[left_rows.index(left)], rights[right_rows.index(right)])
        tile = tile.reshape(shares, part, width)
        out[:, t] = so_far[:, t] + tile if more else tile


def sides(pairs):
    return sorted({left for left, _ in pairs}), sorted({right for _, right in pairs})


def gram(blocks, pairs, shares, so_far=None, cost=0):
    rows, depth = blocks[0][0].shape
    chunks = len(blocks[0])
    flat = [chunk for block in blocks for chunk in block]
    more = so_far is not None
    tiles = len(pairs)
    left_rows, right_rows = sides(pairs)
    inputs = flat + ([so_far] if more else [])
    return pl.pallas_call(
        functools.partial(gram_kernel, pairs, chunks, more),
        in_specs=[pl.BlockSpec(memory_space=pltpu.VMEM)] * len(inputs),
        out_specs=pl.BlockSpec(memory_space=pltpu.VMEM),
        scratch_shapes=[
            pltpu.VMEM((len(side), rows, 3 * chunks * depth), jnp.bfloat16)
            for side in (left_rows, right_rows)
        ],
        out_shape=jax.ShapeDtypeStruct((shares, tiles, rows // shares, rows), jnp.float32),
        cost_estimate=pl.CostEstimate(flops=cost, bytes_accessed=0, transcendentals=0),
        name="gram",
    )(*inputs)


def in_vmem(kernel, inputs, outputs, name, tables=()):
    return pl.pallas_call(
        kernel,
        in_specs=[pl.BlockSpec(memory_space=pltpu.SMEM)] * len(tables)
        + [pl.BlockSpec(memory_space=pltpu.VMEM)] * len(inputs),
        out_specs=[pl.BlockSpec(memory_space=pltpu.VMEM)] * len(outputs),
        out_shape=[jax.ShapeDtypeStruct(shape, jnp.float32) for shape in outputs],
        cost_estimate=pl.CostEstimate(flops=0, bytes_accessed=1 << 20, transcendentals=0),
        name=name,
    )(*tables, *inputs)


def summed(moved, routes):
    def kernel(moved_ref, *outs):
        totals = [moved_ref[:, tile].sum(0) for tile in range(moved_ref.shape[1])]
        for out, (_, as_is, to_turn) in zip(outs, routes):
            for k, tile in enumerate(as_is + to_turn):
                out[k] = totals[tile]

    shape = moved.shape[2:]
    outputs = [(len(as_is + to_turn),) + shape for _, as_is, to_turn in routes]
    return in_vmem(kernel, [moved], outputs, "sum")


def turned(slabs, picks, shares):
    part, width = slabs[0].shape[1:]

    def kernel(*refs):
        *ins, out = refs
        rows = [ref[k] for ref, ks in zip(ins, picks) for k in ks]
        rows += [jnp.zeros((part, width), jnp.float32)] * (width // part - len(rows))
        out[...] = jnp.concatenate(rows, axis=0).T.reshape(out.shape)

    return in_vmem(kernel, slabs, [(shares, width // shares, width)], "turn")[0]


def assembled(table, slabs, picks, crossed, columns):
    shares, part, width = crossed.shape

    def kernel(table_ref, *refs):
        *ins, crossed_ref, out = refs
        pieces = [ref[k] for ref, ks in zip(ins, picks) for k in ks]
        for k in range(columns // width - len(pieces)):
            lanes = slice(k * part, (k + 1) * part)
            pieces.append(jnp.concatenate([crossed_ref[s, :, lanes] for s in range(shares)], axis=1))
        for slot, piece in enumerate(pieces):
            out[:, pl.ds(pl.multiple_of(table_ref[slot] * width, width), width)] = piece

    return in_vmem(kernel, [*slabs, crossed], [(part, columns)], "assemble", [table])[0]


def together(*values):
    return lax.optimization_barrier(values)


def on_device(three_index, coefficients):
    rows, aux, width = three_index.shape
    by_aux = three_index.transpose(1, 0, 2)
    blk = lax.axis_index("blk")
    swap_zh = [(x * ZH + 1 - h, x * ZH + h) for x in range(X) for h in range(ZH)]
    shares = lax.axis_size("col")

    def over_x(part):
        moved = lax.all_to_all(
            part, "col", split_axis=0, concat_axis=0, tiled=True, axis_index_groups=X_GROUPS
        )
        return moved.reshape(X, part.shape[0] // X, rows, width)

    def to_other_half(value):
        return lax.ppermute(value, "col", swap_zh)

    def over_col(tiles):
        return lax.all_to_all(tiles, "col", split_axis=0, concat_axis=0, tiled=True)

    cut = aux - X
    ring = [coefficients.T]
    for step in range(1, X):
        route = [(((t + step) % X) * ZH + h, t * ZH + h) for t in range(X) for h in range(ZH)]
        ring.append(lax.ppermute(ring[0], "col", route))
    first, *ring = together(by_aux[:cut], *ring)
    ring = jnp.stack(ring)
    first_part = over_x(first)
    orbitals = lax.all_gather(ring, "blk", axis=0, tiled=False)
    last, first_part = together(by_aux[cut:], first_part)
    last_part = over_x(last)

    def to_send(part, k):
        return transformed(part, k, orbitals, False, SENT_COST)

    def kept(part, k):
        return transformed(part, k, orbitals, True, KEPT_COST)

    def neighbours(own):
        return fetched(own, other_core), fetched(own, next_row), fetched(own, previous_row)

    arrived_0 = to_other_half(to_send(first_part, 0))
    arrived_1 = to_other_half(to_send(first_part, 1))
    kept_1, arrived_0 = together(kept(first_part, 1), arrived_0)
    own_0 = kept(first_part, 0) + arrived_0
    other_0, below_0, above_0 = neighbours(own_0)
    arrived_2 = to_other_half(to_send(last_part, 0))
    own_1 = kept_1 + arrived_1
    own_2 = kept(last_part, 0) + arrived_2
    other_0, above_0, own_1 = together(other_0, above_0, own_1)
    across_0 = fetched(below_0, over_to_across)
    other_1, below_1, above_1 = neighbours(own_1)
    other_1, above_1, own_2 = together(other_1, above_1, own_2)
    across_0, below_1 = together(across_0, below_1)
    across_1 = fetched(below_1, over_to_across)
    other_2, below_2, above_2 = neighbours(own_2)
    known = [(own_0, own_1), (other_0, other_1), (below_0, below_1), (above_0, above_1)]
    early = gram(known, EARLY, shares)
    other_2, below_2, above_2, across_0, early = together(other_2, below_2, above_2, across_0, early)
    across_2 = fetched(below_2, over_to_across)
    known_2 = [(own_2,), (other_2,), (below_2,), (above_2,)]
    early = gram(known_2, EARLY, shares, early)
    late = gram(known + [(across_0, across_1)], LATE, shares)
    early_moved = over_col(early)
    across_2, late, early = together(across_2, late, early)
    late = gram(known_2 + [(across_2,)], LATE, shares, late, LATE_COST)
    early_moved, late = together(early_moved, late)

    def sent_home(moved, routes):
        return [
            delivered(slab, RELATED[target]) if target else slab
            for slab, (target, _, _) in zip(summed(moved, routes), routes)
        ]

    late_moved, *slabs = together(over_col(late), *sent_home(early_moved, EARLY_ROUTES))
    slabs += sent_home(late_moved, LATE_ROUTES)
    straight = [range(len(as_is)) for _, as_is, _ in ROUTES]
    to_turn = [range(len(as_is), len(as_is + to_turn)) for _, as_is, to_turn in ROUTES]

    def chosen(picks):
        return [slab for slab, ks in zip(slabs, picks) if len(ks)], [ks for ks in picks if len(ks)]

    crossed = over_col(turned(*chosen(to_turn), shares))
    table = lax.dynamic_slice(jnp.asarray(column_table()), (blk, 0), (1, 16))[0]
    return assembled(table, *chosen(straight), crossed, rows * lax.axis_size("blk"))


def solution(mesh):
    return jax.shard_map(
        on_device,
        mesh=mesh,
        in_specs=(P("blk", None, "col"), P("col", "blk")),
        out_specs=P(("blk", "col"), None),
        check_vma=False,
    )
```

```python
import functools

import jax
import jax.numpy as jnp
import numpy as np
from jax import lax
from jax.experimental import pallas as pl
from jax.experimental.pallas import tpu as pltpu
from jax.sharding import PartitionSpec as P

Y, ZL, CORES, X, ZH = 4, 2, 2, 4, 2
X_GROUPS = [[x * ZH + zh for x in range(X)] for zh in range(ZH)]
OWN, OTHER, BELOW, ABOVE, ACROSS = range(5)
EARLY = [(OWN, OWN), (OWN, OTHER), (OWN, BELOW), (OTHER, BELOW), (BELOW, ABOVE)]
LATE = [(OWN, ACROSS), (OTHER, ACROSS), (BELOW, ACROSS), (ABOVE, ACROSS)]
EARLY_ROUTES = [(OWN, [0, 1, 2], []), (OTHER, [3], []), (BELOW, [4], [2, 3]), (ABOVE, [], [4])]
LATE_ROUTES = [(OWN, [0], []), (OTHER, [1], []), (BELOW, [2], []), (ABOVE, [3], []),
               (ACROSS, [], [0, 1, 2, 3])]
ROUTES = EARLY_ROUTES + LATE_ROUTES
LATE_COST = 20_000_000_000
SENT_COST = KEPT_COST = 5_000_000_000


def block_of(y, zl, core):
    return ((y % Y) * ZL + zl % ZL) * CORES + core % CORES


def upper(y):
    return (y % Y) // 2


def itself(y, zl, core):
    return y, zl, core


def other_core(y, zl, core):
    return y, zl, 1 - core


def next_row(y, zl, core):
    return y + 1, zl, core


def previous_row(y, zl, core):
    return y - 1, zl, (core + upper(y)) % 2


def next_across(y, zl, core):
    return y + 1, 1 - zl, (core + zl + upper(y)) % 2


def over_to_across(y, zl, core):
    return y, 1 - zl, (core + zl + upper(y)) % 2


RELATED = [itself, other_core, next_row, previous_row, next_across]


def places():
    return [(y, zl, core) for y in range(Y) for zl in range(ZL) for core in range(CORES)]


def fetched(value, source_of):
    route = [(block_of(*source_of(*at)), block_of(*at)) for at in places()]
    return lax.ppermute(value, "blk", route)


def delivered(value, target_of):
    route = [(block_of(*at), block_of(*target_of(*at))) for at in places()]
    return lax.ppermute(value, "blk", route)


def column_table():
    straight, turned = [], []
    for tiles, routes in ((EARLY, EARLY_ROUTES), (LATE, LATE_ROUTES)):
        for target, as_is, to_turn in routes:
            straight += [(target, tiles[k][1]) for k in as_is]
            turned += [(target, tiles[k][0]) for k in to_turn]
    table = np.zeros((len(places()), len(straight + turned)), np.int32)
    for slot, (target, column) in enumerate(straight + turned):
        for at in places():
            table[block_of(*RELATED[target](*at)), slot] = block_of(*RELATED[column](*at))
    return table


def high_and_low(value):
    high = value.astype(jnp.bfloat16)
    return high, (value - high.astype(jnp.float32)).astype(jnp.bfloat16)


def dot(left, right):
    return lax.dot_general(
        left, right, (((1,), (1,)), ((), ())), preferred_element_type=jnp.float32
    )


def transform_kernel(index, keeps, part, orbitals, out, rows_in, orbitals_in, sems):
    col = lax.axis_index("col")
    place, half = col // ZH, lax.rem(col + (0 if keeps else 1), ZH)
    run, each, width = orbitals_in.shape[1:]
    copies = []
    for k in range(X):
        x = lax.rem(place + k, X)
        copies.append((
            pltpu.make_async_copy(part.at[x, index], rows_in.at[k], sems.at[0, k]),
            pltpu.make_async_copy(
                orbitals.at[pl.ds(half * run, run), k], orbitals_in.at[k], sems.at[1, k]
            ),
        ))
    for of_rows, of_orbitals in copies:
        of_rows.start()
        of_orbitals.start()
    for k, (of_rows, of_orbitals) in enumerate(copies):
        of_rows.wait()
        of_orbitals.wait()
        b_high, b_low = high_and_low(rows_in[k])
        c_high, c_low = high_and_low(orbitals_in[k].reshape(run * each, width))
        term = dot(b_high, c_high) + (dot(b_high, c_low) + dot(b_low, c_high))
        out[...] = out[...] + term if k else term


def transformed(part, index, orbitals, keeps, cost):
    rows, width = part.shape[2:]
    blocks, _, each, _ = orbitals.shape
    run = blocks // ZH
    return pl.pallas_call(
        functools.partial(transform_kernel, index, keeps),
        in_specs=[pl.BlockSpec(memory_space=pl.ANY)] * 2,
        out_specs=pl.BlockSpec(memory_space=pltpu.VMEM),
        out_shape=jax.ShapeDtypeStruct((rows, run * each), jnp.float32),
        scratch_shapes=[
            pltpu.VMEM((X, rows, width), jnp.float32),
            pltpu.VMEM((X, run, each, width), jnp.float32),
            pltpu.SemaphoreType.DMA((2, X)),
        ],
        cost_estimate=pl.CostEstimate(flops=cost, bytes_accessed=0, transcendentals=0),
        name="transform",
    )(part, orbitals)


def gram_kernel(pairs, chunks, more, *refs):
    left_rows, right_rows = sides(pairs)
    count = (1 + max(left_rows + right_rows)) * chunks
    blocks, refs = refs[:count], refs[count:]
    if more:
        so_far, refs = refs[0], refs[1:]
    out, lefts, rights = refs
    depth = blocks[0].shape[1]
    for k, block in enumerate(blocks):
        high, low = high_and_low(block[...])
        row, first = k // chunks, k % chunks * 3
        for ref, rows, order in (
            (lefts, left_rows, (high, high, low)), (rights, right_rows, (high, low, high))
        ):
            if row in rows:
                for piece, value in enumerate(order, first):
                    ref[rows.index(row), :, piece * depth : (piece + 1) * depth] = value

    shares, _, part, width = out.shape
    for t, (left, right) in enumerate(pairs):
        tile = dot(lefts[left_rows.index(left)], rights[right_rows.index(right)])
        tile = tile.reshape(shares, part, width)
        out[:, t] = so_far[:, t] + tile if more else tile


def sides(pairs):
    return sorted({left for left, _ in pairs}), sorted({right for _, right in pairs})


def gram(blocks, pairs, shares, so_far=None, cost=0):
    rows, depth = blocks[0][0].shape
    chunks = len(blocks[0])
    flat = [chunk for block in blocks for chunk in block]
    more = so_far is not None
    tiles = len(pairs)
    left_rows, right_rows = sides(pairs)
    inputs = flat + ([so_far] if more else [])
    return pl.pallas_call(
        functools.partial(gram_kernel, pairs, chunks, more),
        in_specs=[pl.BlockSpec(memory_space=pltpu.VMEM)] * len(inputs),
        out_specs=pl.BlockSpec(memory_space=pltpu.VMEM),
        scratch_shapes=[
            pltpu.VMEM((len(side), rows, 3 * chunks * depth), jnp.bfloat16)
            for side in (left_rows, right_rows)
        ],
        out_shape=jax.ShapeDtypeStruct((shares, tiles, rows // shares, rows), jnp.float32),
        cost_estimate=pl.CostEstimate(flops=cost, bytes_accessed=0, transcendentals=0),
        name="gram",
    )(*inputs)


def in_vmem(kernel, inputs, outputs, name, tables=()):
    return pl.pallas_call(
        kernel,
        in_specs=[pl.BlockSpec(memory_space=pltpu.SMEM)] * len(tables)
        + [pl.BlockSpec(memory_space=pltpu.VMEM)] * len(inputs),
        out_specs=[pl.BlockSpec(memory_space=pltpu.VMEM)] * len(outputs),
        out_shape=[jax.ShapeDtypeStruct(shape, jnp.float32) for shape in outputs],
        cost_estimate=pl.CostEstimate(flops=0, bytes_accessed=1 << 20, transcendentals=0),
        name=name,
    )(*tables, *inputs)


def summed(moved, routes):
    def kernel(moved_ref, *outs):
        for out, (_, as_is, to_turn) in zip(outs, routes):
            for k, tile in enumerate(as_is + to_turn):
                out[k] = moved_ref[:, tile].sum(0)

    shape = moved.shape[2:]
    outputs = [(len(as_is + to_turn),) + shape for _, as_is, to_turn in routes]
    return in_vmem(kernel, [moved], outputs, "sum")


def turned(slabs, picks, shares):
    part, width = slabs[0].shape[1:]

    def kernel(*refs):
        *ins, out = refs
        rows = [ref[k] for ref, ks in zip(ins, picks) for k in ks]
        rows += [jnp.zeros((part, width), jnp.float32)] * (width // part - len(rows))
        out[...] = jnp.concatenate(rows, axis=0).T.reshape(out.shape)

    return in_vmem(kernel, slabs, [(shares, width // shares, width)], "turn")[0]


def assembled(table, slabs, picks, crossed, columns):
    shares, part, width = crossed.shape

    def kernel(table_ref, *refs):
        *ins, crossed_ref, out = refs
        pieces = [ref[k] for ref, ks in zip(ins, picks) for k in ks]
        for k in range(columns // width - len(pieces)):
            lanes = slice(k * part, (k + 1) * part)
            pieces.append(jnp.concatenate([crossed_ref[s, :, lanes] for s in range(shares)], axis=1))
        for slot, piece in enumerate(pieces):
            out[:, pl.ds(pl.multiple_of(table_ref[slot] * width, width), width)] = piece

    return in_vmem(kernel, [*slabs, crossed], [(part, columns)], "assemble", [table])[0]


def together(*values):
    return lax.optimization_barrier(values)


def on_device(three_index, coefficients):
    rows, aux, width = three_index.shape
    by_aux = three_index.transpose(1, 0, 2)
    blk = lax.axis_index("blk")
    swap_zh = [(x * ZH + 1 - h, x * ZH + h) for x in range(X) for h in range(ZH)]
    shares = lax.axis_size("col")

    def over_x(part):
        moved = lax.all_to_all(
            part, "col", split_axis=0, concat_axis=0, tiled=True, axis_index_groups=X_GROUPS
        )
        return moved.reshape(X, part.shape[0] // X, rows, width)

    def to_other_half(value):
        return lax.ppermute(value, "col", swap_zh)

    def over_col(tiles):
        return lax.all_to_all(tiles, "col", split_axis=0, concat_axis=0, tiled=True)

    cut = aux - X
    ring = [coefficients.T]
    for step in range(1, X):
        route = [(((t + step) % X) * ZH + h, t * ZH + h) for t in range(X) for h in range(ZH)]
        ring.append(lax.ppermute(ring[0], "col", route))
    first, *ring = together(by_aux[:cut], *ring)
    ring = jnp.stack(ring)
    first_part = over_x(first)
    orbitals = lax.all_gather(ring, "blk", axis=0, tiled=False)
    last, first_part = together(by_aux[cut:], first_part)
    last_part = over_x(last)

    def to_send(part, k):
        return transformed(part, k, orbitals, False, SENT_COST)

    def kept(part, k):
        return transformed(part, k, orbitals, True, KEPT_COST)

    def neighbours(own):
        return fetched(own, other_core), fetched(own, next_row), fetched(own, previous_row)

    arrived_0 = to_other_half(to_send(first_part, 0))
    arrived_1 = to_other_half(to_send(first_part, 1))
    own_0 = kept(first_part, 0) + arrived_0
    other_0, below_0, above_0 = neighbours(own_0)
    leaving_2, first_part = together(to_send(last_part, 0), first_part)
    arrived_2 = to_other_half(leaving_2)
    own_1 = kept(first_part, 1) + arrived_1
    own_2 = kept(last_part, 0) + arrived_2
    other_0, below_0, above_0, own_1 = together(other_0, below_0, above_0, own_1)
    across_0 = fetched(below_0, over_to_across)
    other_1, below_1, above_1 = neighbours(own_1)
    other_1, above_1, own_2 = together(other_1, above_1, own_2)
    across_0, below_1 = together(across_0, below_1)
    across_1 = fetched(below_1, over_to_across)
    other_2, below_2, above_2 = neighbours(own_2)
    known = [(own_0, own_1), (other_0, other_1), (below_0, below_1), (above_0, above_1)]
    early = gram(known, EARLY, shares)
    other_2, below_2, above_2, across_0, early = together(other_2, below_2, above_2, across_0, early)
    across_2 = fetched(below_2, over_to_across)
    known_2 = [(own_2,), (other_2,), (below_2,), (above_2,)]
    early = gram(known_2, EARLY, shares, early)
    late = gram(known + [(across_0, across_1)], LATE, shares)
    early_moved = over_col(early)
    across_2, late, early = together(across_2, late, early)
    late = gram(known_2 + [(across_2,)], LATE, shares, late, LATE_COST)
    early_moved, late = together(early_moved, late)

    def sent_home(moved, routes):
        return [
            delivered(slab, RELATED[target]) if target else slab
            for slab, (target, _, _) in zip(summed(moved, routes), routes)
        ]

    late_moved, *slabs = together(over_col(late), *sent_home(early_moved, EARLY_ROUTES))
    slabs += sent_home(late_moved, LATE_ROUTES)
    straight = [range(len(as_is)) for _, as_is, _ in ROUTES]
    to_turn = [range(len(as_is), len(as_is + to_turn)) for _, as_is, to_turn in ROUTES]

    def chosen(picks):
        return [slab for slab, ks in zip(slabs, picks) if len(ks)], [ks for ks in picks if len(ks)]

    crossed = over_col(turned(*chosen(to_turn), shares))
    table = lax.dynamic_slice(jnp.asarray(column_table()), (blk, 0), (1, 16))[0]
    return assembled(table, *chosen(straight), crossed, rows * lax.axis_size("blk"))


def solution(mesh):
    return jax.shard_map(
        on_device,
        mesh=mesh,
        in_specs=(P("blk", None, "col"), P("col", "blk")),
        out_specs=P(("blk", "col"), None),
        check_vma=False,
    )
```
